128 devices in a mesh: row: 16 (over y, z_hi, core), col: 8 (over x, z_lo).
Axes of the slice: x: 4, y: 4, z: 4 (z_hi: 2, z_lo: 2; z = z_hi * 2 + z_lo), core: 2. Of those that a mesh axis runs over, the one named last changes fastest.
Arguments:
- anc_inverse: float32 [4096, 4096], P('row', 'col')
- off_factor: float32 [2, 4096, 4096], P(None, 'row', 'col'), may hold values from -0.09375 to 0.09375
- diag_inverse: float32 [2, 4096, 4096], P(None, 'row', 'col')
- block_mask: int32 [2, 32], P(None, 'row'), may hold values 0 or 1
- edge_child: int32 [2, 32768], P(None, ('row', 'col')), may hold values from 0 to 4095, as said below
- edge_other: int32 [2, 32768], P(None, ('row', 'col')), may hold values from 0 to 8191, as said below
Outputs:
- off_inverse: float32 [2, 4096, 4096], P(None, 'row', 'col')
- diag_part: float32 [2, 4096, 4096], P(None, 'row', 'col')
- resist: float32 [2, 32768], P(None, ('row', 'col'))
The draws below stay inside these ranges and needn't reach their ends.
Inputs may be any that keep to these rules, and one draw needn't show every extreme that they name: `edge_child`: edges come in runs of 256; run d, with c = d % 8, has u in [c * 4096 / 8, (c + 1) * 4096 / 8). `edge_other`: in run d of 256 edges, with r = d // 8, v lies in [r * 4096 / 16, (r + 1) * 4096 / 16) or in 4096 + [r * 4096 / 16, (r + 1) * 4096 / 16); v never equals u.
All inputs are finite; a program needn't handle non-finite values. No bound on the sum of `block_mask` on one device may be relied on, other than what follows from the above.
Results may differ from the reference program's by a relative error of at most 0.000073.
Values sent between devices are 32-bit elements; how exact they have to be, the bound alone decides.
A program may use at most 128 MiB of HBM per device.

```python
import math
import jax
import jax.numpy as jnp
from jax import lax

ANCESTOR = 4096
SUPERCOLS = 4096
FRONTS = 2
BLOCK = 128
EDGE_DEV = 256
N_ROW = 16
N_COL = 8


def dominant(key, lead, order):
    key_off, key_diag = jax.random.split(key, 2)
    spread = jax.random.normal(key_off, (lead, order, order), jnp.float32)
    spread = (spread + jnp.swapaxes(spread, 1, 2)) * (0.5 / math.sqrt(order))
    diagonal = jnp.exp(jax.random.uniform(key_diag, (lead, order), jnp.float32, 0.0, math.log(4.0)))
    identity = jnp.eye(order, dtype=jnp.float32)
    return spread * (1.0 - identity) + identity * diagonal[:, None, :]


def draw_anc_inverse(key, part):
    return dominant(jax.random.fold_in(key, 11), 1, ANCESTOR)[0]


def draw_diag_inverse(key, part):
    return dominant(jax.random.fold_in(key, 13), FRONTS, SUPERCOLS)


def edge_pair(key):
    base = jax.random.fold_in(key, 29)
    key_u, key_kind, key_child, key_anc = jax.random.split(base, 4)
    total = EDGE_DEV * N_ROW * N_COL
    position = jnp.arange(total, dtype=jnp.int32)
    run_id = position // EDGE_DEV
    row_id = run_id // N_COL
    col_id = run_id % N_COL
    col_width = SUPERCOLS // N_COL
    row_width = SUPERCOLS // N_ROW
    anc_width = ANCESTOR // N_ROW
    shape = (FRONTS, total)
    near = col_id * col_width + jax.random.randint(key_u, shape, 0, col_width, dtype=jnp.int32)
    kind = jax.random.randint(key_kind, shape, 0, 2, dtype=jnp.int32)
    child_end = row_id * row_width + jax.random.randint(key_child, shape, 0, row_width, dtype=jnp.int32)
    child_end = jnp.where(child_end == near, row_id * row_width + (child_end - row_id * row_width + 1) % row_width, child_end)
    anc_end = SUPERCOLS + row_id * anc_width + jax.random.randint(key_anc, shape, 0, anc_width, dtype=jnp.int32)
    far = jnp.where(kind == 0, child_end, anc_end)
    return (near.astype(jnp.int32), far.astype(jnp.int32))


def draw_edge_child(key, part):
    return edge_pair(key)[0]


def draw_edge_other(key, part):
    return edge_pair(key)[1]


def set_ends(result, stream_key, least, high):
    index_at = [jax.random.randint(jax.random.fold_in(stream_key, axis), (), 0, length) for axis, length in enumerate(result.shape)]
    widest = result.shape.index(max(result.shape))
    neighbour = index_at[:widest] + [(index_at[widest] + 1) % result.shape[widest]] + index_at[widest + 1:]
    return result.at[tuple(index_at)].set(least).at[tuple(neighbour)].set(high)


def levels(key, shape, shards, least, top_value):
    level = 1.0
    for dim, shards_of in shards:
        steps = jax.random.uniform(jax.random.fold_in(jax.random.fold_in(key, 6), dim), (shards_of,), jnp.float32, least / len(shards), top_value / len(shards))
        level = level * jnp.repeat(jnp.exp(steps), shape[dim] // shards_of).reshape((-1,) + (1,) * (len(shape) - 1 - dim))
    return level


def centred(stream_key, shape, scale, limit, cuts=(), kind=jnp.bfloat16):
    level = levels(stream_key, shape, cuts, -0.22, 0.18) if cuts else 1.0
    entries = jax.random.normal(stream_key, shape, jnp.float32) * scale * level
    return jnp.minimum(jnp.maximum(entries, -limit), limit).astype(kind)


def setup_inputs(seed: int = 0) -> dict:
    splits = jax.random.split(jax.random.key(seed), 7)
    anc_inverse = draw_anc_inverse(jax.random.fold_in(splits[6], 71), 0)
    off_factor = centred(splits[1], (FRONTS, ANCESTOR, SUPERCOLS), ANCESTOR ** -0.5, 0.09375, ((1, 16), (2, 8)), jnp.float32)
    diag_inverse = draw_diag_inverse(jax.random.fold_in(splits[6], 71), 0)
    block_mask = set_ends((jax.random.randint(splits[3], (FRONTS, ANCESTOR // BLOCK), 0, 4) < 3).astype(jnp.int32), jax.random.fold_in(splits[3], 1), 0, 1)
    edge_child = draw_edge_child(jax.random.fold_in(splits[6], 71), 0)
    edge_other = draw_edge_other(jax.random.fold_in(splits[6], 71), 0)
    return {"anc_inverse": anc_inverse, "off_factor": off_factor, "diag_inverse": diag_inverse, "block_mask": block_mask, "edge_child": edge_child, "edge_other": edge_other}


def reference(anc_inverse, off_factor, diag_inverse, block_mask, edge_child, edge_other):
    keep = jnp.repeat(block_mask, BLOCK, axis=1).astype(jnp.float32)
    factor = off_factor * keep[:, :, None]
    off_inverse = -jnp.einsum("ab,kbi->kai", anc_inverse, factor, precision=lax.Precision.HIGHEST)
    diag_part = diag_inverse - jnp.einsum("kaj,kai->kji", off_inverse, factor, precision=lax.Precision.HIGHEST)
    cc_diag = jnp.diagonal(diag_part, axis1=1, axis2=2)
    z_diag = jnp.diagonal(anc_inverse)
    is_child = edge_other < SUPERCOLS
    child_v = jnp.clip(edge_other, 0, SUPERCOLS - 1).astype(jnp.int32)
    anc_v = jnp.clip(edge_other - SUPERCOLS, 0, ANCESTOR - 1).astype(jnp.int32)
    fronts = jnp.arange(FRONTS).astype(jnp.int32)[:, None]
    mixed = jnp.where(is_child, diag_part[fronts, child_v, edge_child], off_inverse[fronts, anc_v, edge_child])
    near = jnp.take_along_axis(cc_diag, edge_child, axis=1)
    far = jnp.where(is_child, jnp.take_along_axis(cc_diag, child_v, axis=1), z_diag[anc_v])
    resist = near + far - 2.0 * mixed
    return off_inverse, diag_part, resist
```

```python
import functools

import jax
import jax.numpy as jnp
from jax import lax
from jax.experimental import pallas as pl
from jax.experimental.pallas import tpu as pltpu
from jax.sharding import PartitionSpec as P

MESH = pl.DeviceIdType.MESH
CHUNKS = 2


def place():
    row = lax.axis_index("row")
    col = lax.axis_index("col")
    return lax.div(col, 2), lax.div(row, 4), lax.rem(lax.div(row, 2), 2), lax.rem(col, 2), lax.rem(row, 2)


def at(x, y, z, k):
    x, y, z, k = lax.rem(x, 4), lax.rem(y, 4), lax.rem(z, 4), lax.rem(k, 2)
    return (y * 4 + lax.div(z, 2) * 2 + k, x * 2 + lax.rem(z, 2))


def partners(x, y, h, l, k):
    found = {}
    for dh in range(2):
        for dl in range(2):
            for dk in range(2):
                found[(0, 0, dh, dl, dk)] = None
    for d in (1, 3):
        found[(d, 0, 0, 0, 0)] = None
    for dy in range(4):
        for dh in range(2):
            for dk in range(2):
                found[(0, dy, dh, 0, dk)] = None
    for dx in range(4):
        for dl in range(2):
            found[(dx, 0, 0, dl, 0)] = None
    del found[(0, 0, 0, 0, 0)]
    ids = []
    for dx, dy, dh, dl, dk in found:
        z = 2 * lax.rem(h + dh, 2) + lax.rem(l + dl, 2)
        ids.append(at(x + dx, y + dy, z, k + dk))
    return ids


def split(value):
    high = value.astype(jnp.bfloat16)
    return high, (value - high.astype(jnp.float32)).astype(jnp.bfloat16)


def dot3(left_high, left_low, right_high, right_low):
    def dot(left, right):
        return jnp.dot(left, right, preferred_element_type=jnp.float32)

    return dot(left_high, right_high) + (dot(left_high, right_low) + dot(left_low, right_high))


def kernel(
    u,
    mask_ref,
    anc_ref,
    fac_ref,
    diag_ref,
    z_out,
    g_out,
    near_out,
    far_out,
    f_send,
    f_all,
    f_high,
    f_low,
    a_send,
    a_all,
    a_high,
    a_low,
    p1,
    far1,
    near1,
    z_own,
    z_turn,
    z_all,
    zh,
    zl,
    p2,
    far2,
    near2,
    g_own,
    d_send,
    send_sems,
    recv_sems,
):
    x, y, h, l, k = place()
    z = 2 * h + l
    rows = 2 * u
    f32 = jnp.float32

    count = [0]

    def fresh(n=1):
        first = count[0]
        count[0] += n
        return first

    def mult(value, of):
        return pl.multiple_of(value, of)

    def remote(src, dst, device, send, recv):
        return pltpu.make_async_remote_copy(
            src_ref=src,
            dst_ref=dst,
            send_sem=send_sems.at[send],
            recv_sem=recv_sems.at[recv],
            device_id=device,
            device_id_type=MESH,
        )

    sent = []

    def push(src, dst, device):
        i = fresh()
        copy = remote(src, dst, device, i, i)
        copy.start()
        sent.append(copy)
        return copy

    barrier = pltpu.get_barrier_semaphore()
    greet = partners(x, y, h, l, k)
    for device in greet:
        pl.semaphore_signal(barrier, inc=1, device_id=device, device_id_type=MESH)

    sibling = at(x, y, z, k + 1)
    x_right, x_left = at(x + 1, y, z, k), at(x + 3, y, z, k)
    y_right, y_left = at(x, y + 1, z, k), at(x, y + 3, z, k)
    z_right, z_left = at(x, y, z + 1, k), at(x, y, z + 3, k)
    other = 1 - k

    def f_place(j, zz, half):
        row = (lax.div(zz, 2) * 2 + half) * rows
        return f_all.at[j, pl.ds(mult(row, rows), rows), pl.ds(mult(lax.rem(zz, 2) * 2 * u, 2 * u), 2 * u)]

    for j in range(CHUNKS):
        for b in range(2):
            for part in range(2):
                source = pl.ds(b * u, u)
                lanes = pl.ds(part * 2 * u + j * u, u)
                mine = fac_ref[k, source, lanes] * mask_ref[k, b].astype(f32)
                theirs = fac_ref[other, source, lanes] * mask_ref[other, b].astype(f32)
                f_place(j, z, k).at[pl.ds(b * u, u), pl.ds(part * u, u)][...] = mine
                f_send[j, pl.ds(b * u, u), pl.ds(part * u, u)] = theirs

    def a_place(xx, hh, kk):
        return a_all.at[lax.rem(xx, 4), :, pl.ds(mult((hh * 2 + kk) * rows, rows), rows)]

    a_place(x, h, k)[...] = jnp.transpose(anc_ref[:, pl.ds(mult(h * rows, rows), rows)])
    a_send[...] = jnp.transpose(anc_ref[:, pl.ds(mult((1 - h) * rows, rows), rows)])

    pl.semaphore_wait(barrier, len(greet))

    f_pair = [None] * CHUNKS
    f_near = [None] * CHUNKS

    def start_pair(j):
        f_pair[j] = push(f_send.at[j], f_place(j, z, k), sibling)

    def ring_half(src_place, right, left):
        return push(src_place, src_place, right), push(src_place, src_place, left)

    def start_near(j):
        own = ring_half(f_place(j, z, k), z_right, z_left)
        f_pair[j].wait_recv()
        pair = ring_half(f_place(j, z, other), z_right, z_left)
        f_near[j] = (own, pair)

    def forward(j):
        own, pair = f_near[j]
        own[0].wait_recv()
        pair[0].wait_recv()
        to_right = push(f_place(j, lax.rem(z + 3, 4), 0), f_place(j, lax.rem(z + 3, 4), 0), z_right)
        own[1].wait_recv()
        pair[1].wait_recv()
        to_left = push(f_place(j, lax.rem(z + 1, 4), 1), f_place(j, lax.rem(z + 1, 4), 1), z_left)
        return to_right, to_left

    start_pair(0)
    f_own0 = ring_half(f_place(0, z, k), z_right, z_left)
    a_pair = push(a_send, a_place(x, h, k), at(x, y, z + 2, k))
    a_own = ring_half(a_place(x, h, k), x_right, x_left)
    a_sib = [push(a_place(x, h, k), a_place(x, h, k), sibling)]
    f_pair[0].wait_recv()
    f_near[0] = (f_own0, ring_half(f_place(0, z, other), z_right, z_left))
    start_pair(1)
    a_pair.wait_recv()
    a_mate = ring_half(a_place(x, 1 - h, k), x_right, x_left)
    a_sib.append(push(a_place(x, 1 - h, k), a_place(x, 1 - h, k), sibling))
    f_far = forward(0)
    a_own[0].wait_recv()
    a_mate[0].wait_recv()
    a_far = [push(a_place(x + 3, 0, k), a_place(x + 3, 0, k), x_right)]
    a_own[1].wait_recv()
    a_mate[1].wait_recv()
    a_far.append(push(a_place(x + 1, 1, k), a_place(x + 1, 1, k), x_left))
    for xx in (x + 3, x + 1):
        for hh in range(2):
            a_sib.append(push(a_place(xx, hh, k), a_place(xx, hh, k), sibling))
    start_near(1)
    f_far[0].wait_recv()
    f_far[1].wait_recv()
    f_high[0], f_low[0] = split(f_all[0])
    a_far[0].wait_recv()
    a_far[1].wait_recv()
    for hh in range(2):
        a_sib.append(push(a_place(x + 2, hh, k), a_place(x + 2, hh, k), sibling))
    for copy in a_sib:
        copy.wait_recv()
    for xx in range(4):
        a_high[xx], a_low[xx] = split(a_all[xx])

    def reduce_scatter(j, product, part, far, near, height):
        half = height // 2
        upper, lower = pl.ds(0, half), pl.ds(half, half)
        product(2)
        out = [
            push(part.at[j, 2, upper], far.at[j, 0], y_right),
            push(part.at[j, 2, lower], far.at[j, 1], y_left),
        ]
        product(1)
        out.append(push(part.at[j, 1, lower], near.at[j, 0, lower], y_right))
        product(3)
        out.append(push(part.at[j, 3, upper], near.at[j, 1, upper], y_left))
        product(0)

        def add():
            out[0].wait_recv()
            part[j, 1, upper] = part[j, 1, upper] + far[j, 0]
            out.append(push(part.at[j, 1, upper], near.at[j, 0, upper], y_right))
            out[1].wait_recv()
            part[j, 3, lower] = part[j, 3, lower] + far[j, 1]
            out.append(push(part.at[j, 3, lower], near.at[j, 1, lower], y_left))

        def total():
            for copy in out[2:]:
                copy.wait_recv()
            return part[j, 0] + near[j, 0] + near[j, 1]

        return add, total

    def stage1(j):
        def product(d):
            block = lax.rem(y + d, 4)
            p1[j, d] = dot3(a_high[block], a_low[block], f_high[j], f_low[j])

        return reduce_scatter(j, product, p1, far1, near1, rows)

    z_first = fresh(4 * CHUNKS)
    z_send = fresh(4 * CHUNKS)
    z_moves = []

    def stays(out_lane):
        return jnp.logical_and(jnp.logical_and(l == h, k == h), l == out_lane)

    def place_out(src, dst, lane, send, recv):
        here = stays(lane)
        copy = remote(src, dst, at(x, y, 2 * l + lane, h), send, recv)
        local = pltpu.make_async_copy(src, dst, recv_sems.at[recv])

        @pl.when(here)
        def _():
            local.start()

        @pl.when(jnp.logical_not(here))
        def _():
            copy.start()

        return here, copy

    def z_place(j, xx, zz):
        position = lax.rem(zz, 2) * 2 + lax.div(zz, 2)
        return z_all.at[j, lax.rem(xx, 4), :, pl.ds(mult(position * rows, rows), rows)]

    def z_finish(j, total):
        z_own[j] = -total()
        for lane in range(2):
            for part in range(2):
                z_turn[j, part * 2 + lane] = jnp.transpose(z_own[j, :, pl.ds((lane * 2 + part) * u, u)])
        z_place(j, x, z)[...] = z_turn[j, z]
        swap = []
        for d in (2, 1, 3):
            target = lax.rem(z + d, 4)
            swap.append(push(z_turn.at[j, target], z_place(j, x, z), at(x, y, target, k)))
        return swap

    def z_result(j):
        for lane in range(2):
            for part in range(2):
                z_moves.append(
                    place_out(
                        z_own.at[j, :, pl.ds((lane * 2 + part) * u, u)],
                        z_out.at[k, :, pl.ds(part * 2 * u + j * u, u)],
                        lane,
                        z_send + (j * 2 + lane) * 2 + part,
                        z_first + (k * CHUNKS + j) * 2 + part,
                    )
                )

    def z_half(j, xx, half):
        return z_all.at[j, lax.rem(xx, 4), :, pl.ds(half * 4 * u, 4 * u)]

    def z_near(j, swap):
        for copy in swap:
            copy.wait_recv()
        return [ring_half(z_half(j, x, half), x_right, x_left) for half in range(2)]

    def z_forward(j, near):
        near[0][0].wait_recv()
        to_right = push(z_half(j, x + 3, 0), z_half(j, x + 3, 0), x_right)
        near[1][1].wait_recv()
        to_left = push(z_half(j, x + 1, 1), z_half(j, x + 1, 1), x_left)
        return to_right, to_left

    def z_gathered(j, near, far):
        near[1][0].wait_recv()
        near[0][1].wait_recv()
        far[0].wait_recv()
        far[1].wait_recv()
        for xx in range(4):
            zh[j, xx], zl[j, xx] = split(z_all[j, xx])

    def stage2(j):
        def product(d):
            block = lax.rem(y + d, 4)
            for q in range(CHUNKS):
                value = dot3(zh[j, block], zl[j, block], f_high[q], f_low[q])
                for piece in range(4):
                    lanes = (piece // 2) * 4 * u + (piece % 2) * 2 * u + q * u
                    p2[j, d, :, pl.ds(lanes, u)] = value[:, piece * u : (piece + 1) * u]

        return reduce_scatter(j, product, p2, far2, near2, u)

    g_first = fresh(2 * CHUNKS)
    g_send = fresh(2 * CHUNKS)
    g_moves = []

    def g_finish(j, total):
        g_own[j] = total()
        for lane in range(2):
            g_moves.append(
                place_out(
                    g_own.at[j, :, pl.ds(lane * 4 * u, 4 * u)],
                    g_out.at[k, pl.ds(j * u, u), :],
                    lane,
                    g_send + j * 2 + lane,
                    g_first + k * CHUNKS + j,
                )
            )

    add10, total10 = stage1(0)
    f_far1 = forward(1)
    add10()
    f_far1[0].wait_recv()
    f_far1[1].wait_recv()
    f_high[1], f_low[1] = split(f_all[1])
    add11, total11 = stage1(1)
    swap0 = z_finish(0, total10)
    add11()
    near0 = z_near(0, swap0)
    z_result(0)
    fore0 = z_forward(0, near0)
    swap1 = z_finish(1, total11)
    z_gathered(0, near0, fore0)
    near1_ = z_near(1, swap1)
    z_result(1)
    add20, total20 = stage2(0)
    fore1 = z_forward(1, near1_)
    add20()
    z_gathered(1, near1_, fore1)
    add21, total21 = stage2(1)
    g_finish(0, total20)
    add21()
    g_finish(1, total21)

    for front in range(2):
        for j in range(CHUNKS):
            for part in range(2):
                here = z_out.at[front, :, pl.ds(part * 2 * u + j * u, u)]
                pltpu.make_async_copy(here, here, recv_sems.at[z_first + (front * CHUNKS + j) * 2 + part]).wait()
            here = g_out.at[front, pl.ds(j * u, u), :]
            pltpu.make_async_copy(here, here, recv_sems.at[g_first + front * CHUNKS + j]).wait()

    d_send[...] = jnp.zeros_like(d_send)
    eye = lax.broadcasted_iota(jnp.int32, (rows, rows), 0) == lax.broadcasted_iota(jnp.int32, (rows, rows), 1)
    own_lanes = pl.ds(mult(k * rows, rows), rows)
    for front in range(2):
        g_out[front] = diag_ref[front] - g_out[front]
        d_send[pl.ds(front, 1)] = jnp.sum(jnp.where(eye, g_out[front, :, own_lanes], 0.0), axis=0, keepdims=True)
    d_send[pl.ds(2, 1)] = jnp.sum(jnp.where(eye, anc_ref[:, own_lanes], 0.0), axis=0, keepdims=True)

    holds = jnp.logical_and(x == y, l == h)
    near_recv = fresh(2)
    far_recv = fresh(1)
    d_first = fresh(24)
    d_copies = []
    for dy in range(4):
        for dh in range(2):
            for dk in range(2):
                if dy or dh or dk:
                    device = at(x, y + dy, 2 * lax.rem(h + dh, 2) + l, k + dk)
                    d_copies.append(remote(d_send, near_out.at[k], device, d_first + len(d_copies), near_recv + k))
    for dx in range(4):
        for dl in range(2):
            if dx or dl:
                device = at(x + dx, y, 2 * h + lax.rem(l + dl, 2), k)
                d_copies.append(remote(d_send, far_out, device, d_first + len(d_copies), far_recv))

    @pl.when(holds)
    def _():
        for copy in d_copies:
            copy.start()
        pltpu.make_async_copy(d_send, near_out.at[k], recv_sems.at[near_recv + k]).start()
        pltpu.make_async_copy(d_send, far_out, recv_sems.at[far_recv]).start()

    for core in range(2):
        pltpu.make_async_copy(near_out.at[core], near_out.at[core], recv_sems.at[near_recv + core]).wait()
    pltpu.make_async_copy(far_out, far_out, recv_sems.at[far_recv]).wait()

    @pl.when(holds)
    def _():
        for copy in d_copies:
            copy.wait_send()

    for here, copy in z_moves + g_moves:

        @pl.when(jnp.logical_not(here))
        def _():
            copy.wait_send()

    for copy in sent:
        copy.wait_send()


SEMAPHORES = 192


def per_device(anc_inverse, off_factor, diag_inverse, block_mask, edge_child, edge_other):
    fronts, rows, width = off_factor.shape
    u = rows // 2
    n = CHUNKS
    f32, bf16 = jnp.float32, jnp.bfloat16
    vmem = pl.BlockSpec(memory_space=pltpu.VMEM)
    scratch = [
        ((n, rows, 2 * u), f32),
        ((n, 8 * u, 4 * u), f32),
        ((n, 8 * u, 4 * u), bf16),
        ((n, 8 * u, 4 * u), bf16),
        ((rows, rows), f32),
        ((4, rows, 8 * u), f32),
        ((4, rows, 8 * u), bf16),
        ((4, rows, 8 * u), bf16),
        ((n, 4, rows, 4 * u), f32),
        ((n, 2, u, 4 * u), f32),
        ((n, 2, rows, 4 * u), f32),
        ((n, rows, 4 * u), f32),
        ((n, 4, u, rows), f32),
        ((n, 4, u, 8 * u), f32),
        ((n, 4, u, 8 * u), bf16),
        ((n, 4, u, 8 * u), bf16),
        ((n, 4, u, 8 * u), f32),
        ((n, 2, u // 2, 8 * u), f32),
        ((n, 2, u, 8 * u), f32),
        ((n, u, 8 * u), f32),
        ((8, rows), f32),
    ]
    flops = 2 * 3 * 2 * (8 * u) ** 3
    off_inverse, diag_part, near_diag, far_diag = pl.pallas_call(
        functools.partial(kernel, u),
        out_shape=(
            jax.ShapeDtypeStruct(off_factor.shape, f32),
            jax.ShapeDtypeStruct(diag_inverse.shape, f32),
            jax.ShapeDtypeStruct((2, 8, rows), f32),
            jax.ShapeDtypeStruct((8, rows), f32),
        ),
        in_specs=[pl.BlockSpec(memory_space=pltpu.SMEM), vmem, vmem, vmem],
        out_specs=(vmem, vmem, vmem, vmem),
        scratch_shapes=[pltpu.VMEM(*entry) for entry in scratch]
        + [pltpu.SemaphoreType.DMA((SEMAPHORES,)), pltpu.SemaphoreType.DMA((SEMAPHORES,))],
        compiler_params=pltpu.CompilerParams(collective_id=0, has_side_effects=True, vmem_limit_bytes=60 << 20),
        cost_estimate=pl.CostEstimate(flops=flops, bytes_accessed=5 << 20, transcendentals=0),
    )(block_mask, anc_inverse, off_factor, diag_inverse)

    supercols = width * lax.axis_size("col")
    row_start = lax.axis_index("row") * rows
    near_at = edge_child - lax.axis_index("col") * width
    is_child = edge_other < supercols
    far_at = jnp.where(is_child, edge_other - row_start, edge_other - supercols - row_start + rows)
    near_hot = (near_at[:, :, None] == jnp.arange(width, dtype=jnp.int32)).astype(f32)
    far_hot = (far_at[:, :, None] == jnp.arange(2 * rows, dtype=jnp.int32)).astype(f32)
    near_table = jnp.concatenate([near_diag[0, :2], near_diag[1, :2]], axis=1)
    far_table = jnp.concatenate([far_diag[:2], jnp.broadcast_to(far_diag[2:3], (fronts, rows))], axis=1)
    both = jnp.concatenate([diag_part, off_inverse], axis=1)
    picked = jnp.einsum("ker,krc->kec", far_hot, both, precision=lax.Precision.HIGHEST)
    resist = jnp.sum(near_hot * (near_table[:, None, :] - 2.0 * picked), axis=2) + jnp.sum(
        far_hot * far_table[:, None, :], axis=2
    )
    return (off_inverse, diag_part, resist)


def solution(mesh):
    placed = (
        P("row", "col"),
        P(None, "row", "col"),
        P(None, "row", "col"),
        P(None, "row"),
        P(None, ("row", "col")),
        P(None, ("row", "col")),
    )
    return jax.shard_map(
        per_device,
        mesh=mesh,
        in_specs=placed,
        out_specs=(P(None, "row", "col"), P(None, "row", "col"), P(None, ("row", "col"))),
        check_vma=False,
    )
```

```python
import functools

import jax
import jax.numpy as jnp
from jax import lax
from jax.experimental import pallas as pl
from jax.experimental.pallas import tpu as pltpu
from jax.sharding import PartitionSpec as P

MESH = pl.DeviceIdType.MESH
CHUNKS = 4
SEMAPHORES = 256

ORDER = (
    "Ap", "Ao", "Am", "Fo0", "Fp0", "Fp1", "Fm0", "Fo1", "Af", "Fm1", "Ff0", "Fp3", "At", "Fo3", "Fm3", "Fd0", "Ad", "Ds", "M10", "M1r0", "Fp2", "Ff1", "Ff3",
    "R1a0", "Fo2", "Fd1", "M11", "T10", "M1r1", "R1a1", "Fd3", "Fm2", "M13", "Zn0", "Ff2", "M1r3", "T11", "Zf0", "R1a3", "Fd2", "M12", "Zn1", "Zo1", "Zd0",
    "M1r2", "Ed", "R1a2", "T13", "Zf1", "M20", "M2r0", "Zn3", "Zd1", "M21", "T12", "Ca", "R2a0", "M2r1", "Cb", "Zf3", "R2a1", "Cc", "Zn2", "Zd3", "Cd", "Zo3",
    "M23", "Ce", "Zf2", "M2r3", "Zo2", "T20", "R2a3", "Zd2", "Zo0", "M22", "T23", "M2r2", "T21", "R2a2", "T22",
)


def place():
    row = lax.axis_index("row")
    col = lax.axis_index("col")
    return lax.div(col, 2), lax.div(row, 4), lax.rem(lax.div(row, 2), 2), lax.rem(col, 2), lax.rem(row, 2)


def at(x, y, z, k):
    x, y, z, k = lax.rem(x, 4), lax.rem(y, 4), lax.rem(z, 4), lax.rem(k, 2)
    return (y * 4 + lax.div(z, 2) * 2 + k, x * 2 + lax.rem(z, 2))


def split(value):
    high = value.astype(jnp.bfloat16)
    return high, (value - high.astype(jnp.float32)).astype(jnp.bfloat16)


def dot3(left_high, left_low, right_high, right_low):
    def dot(left, right):
        return jnp.dot(left, right, preferred_element_type=jnp.float32)

    return dot(left_high, right_high) + (dot(left_high, right_low) + dot(left_low, right_high))


def pick(value, hot):
    high, rest = split(value)
    low = value - high.astype(jnp.float32) - rest.astype(jnp.float32)
    parts = (high, rest, low.astype(jnp.bfloat16))
    return sum(jnp.dot(part, hot, preferred_element_type=jnp.float32) for part in parts)


def weave(first, second):
    half = first.shape[1] // 2
    low = lax.broadcasted_iota(jnp.int32, first.shape, 1) < half
    return (
        jnp.where(low, first, pltpu.roll(second, half, 1)),
        jnp.where(low, pltpu.roll(first, half, 1), second),
    )


def kernel(
    u,
    mask_ref,
    anc_ref,
    fac_ref,
    diag_ref,
    near_ref,
    far_ref,
    z_out,
    g_out,
    r_out,
    f_send,
    f_all,
    f_high,
    f_low,
    a_send,
    a_all,
    a_high,
    a_low,
    p1,
    far1,
    near1,
    z_own,
    z_turn,
    z_all,
    zh,
    zl,
    z_stage,
    p2,
    far2,
    near2,
    g_own,
    g_stage,
    dd_send,
    dd_recv,
    c_part,
    c_plane,
    c_line,
    c_front,
    c_all,
    zd,
    table,
    hot_near,
    hot_far,
    r_part,
    send_sems,
    recv_sems,
):
    x, y, h, l, k = place()
    z = 2 * h + l
    rows = 2 * u
    w = u // 2
    f32 = jnp.float32
    other = 1 - k

    count = [0]

    def fresh(n=1):
        first = count[0]
        count[0] += n
        return first

    def mult(value, of):
        return pl.multiple_of(value, of)

    def remote(src, dst, device, send, recv):
        return pltpu.make_async_remote_copy(
            src_ref=src,
            dst_ref=dst,
            send_sem=send_sems.at[send],
            recv_sem=recv_sems.at[recv],
            device_id=device,
            device_id_type=MESH,
        )

    sent = []

    def push(src, dst, device):
        i = fresh()
        copy = remote(src, dst, device, i, i)
        copy.start()
        sent.append(copy)
        return copy

    sibling = at(x, y, z, k + 1)
    x_right, x_left = at(x + 1, y, z, k), at(x + 3, y, z, k)
    y_right, y_left = at(x, y + 1, z, k), at(x, y + 3, z, k)
    z_right, z_left = at(x, y, z + 1, k), at(x, y, z + 3, k)
    z_across = at(x, y, z + 2, k)
    z_mate = at(x, y, 2 * h + 1 - l, k)

    barrier = pltpu.get_barrier_semaphore()
    greet = (z_across, sibling, x_right, x_left, z_right, z_left, y_right, y_left)
    for device in greet:
        pl.semaphore_signal(barrier, inc=1, device_id=device, device_id_type=MESH)

    own_lanes = pl.ds(mult(k * rows, rows), rows)

    def a_place(xx, hh, kk):
        return a_all.at[lax.rem(xx, 4), :, pl.ds(mult((hh * 2 + kk) * rows, rows), rows)]

    a_send[...] = jnp.transpose(anc_ref[:, pl.ds(mult((1 - h) * rows, rows), rows)])
    a_place(x, h, k)[...] = jnp.transpose(anc_ref[:, pl.ds(mult(h * rows, rows), rows)])

    def f_place(j, zz, half):
        row = (lax.div(zz, 2) * 2 + half) * rows
        return f_all.at[j, pl.ds(mult(row, rows), rows), pl.ds(mult(lax.rem(zz, 2) * u, u), u)]

    def mask_factor():
        for front, mine in ((other, False), (k, True)):
            for b in range(2):
                source = pl.ds(b * u, u)
                keep = mask_ref[front, b].astype(f32)
                for pair in range(2):
                    woven = weave(
                        fac_ref[front, source, pl.ds(pair * u, u)] * keep,
                        fac_ref[front, source, pl.ds((2 + pair) * u, u)] * keep,
                    )
                    for i in range(2):
                        if mine:
                            f_place(2 * pair + i, z, k).at[source][...] = woven[i]
                        else:
                            f_send[2 * pair + i, source] = woven[i]

    got = {}

    def ring_half(name, src, right, left):
        got[name + "+"] = push(src, src, right)
        got[name + "-"] = push(src, src, left)

    def wait(*names):
        for name in names:
            got[name].wait_recv()

    def to_sibling(xx, hh):
        got[f"As{len([n for n in got if n.startswith('As')])}"] = push(a_place(xx, hh, k), a_place(xx, hh, k), sibling)

    def do_ap():
        got["Ap"] = push(a_send, a_place(x, h, k), z_across)

    def do_ao():
        ring_half("Ao", a_place(x, h, k), x_right, x_left)
        to_sibling(x, h)

    def do_am():
        wait("Ap")
        ring_half("Am", a_place(x, 1 - h, k), x_right, x_left)
        to_sibling(x, 1 - h)

    def do_af():
        wait("Ao+", "Am+")
        got["Af+"] = push(a_place(x + 3, 0, k), a_place(x + 3, 0, k), x_right)
        wait("Ao-", "Am-")
        got["Af-"] = push(a_place(x + 1, 1, k), a_place(x + 1, 1, k), x_left)
        for xx in (x + 3, x + 1):
            for hh in range(2):
                to_sibling(xx, hh)

    def do_at():
        wait("Af+", "Af-")
        for hh in range(2):
            to_sibling(x + 2, hh)

    def do_ad():
        for i in range(8):
            wait(f"As{i}")
        for xx in range(4):
            a_high[xx], a_low[xx] = split(a_all[xx])

    def do_fp(j):
        got[f"Fp{j}"] = push(f_send.at[j], f_place(j, z, k), sibling)

    def do_fo(j):
        ring_half(f"Fo{j}", f_place(j, z, k), z_right, z_left)

    def do_fm(j):
        wait(f"Fp{j}")
        ring_half(f"Fm{j}", f_place(j, z, other), z_right, z_left)

    def do_ff(j):
        wait(f"Fo{j}+", f"Fm{j}+")
        got[f"Ff{j}+"] = push(f_place(j, lax.rem(z + 3, 4), 0), f_place(j, lax.rem(z + 3, 4), 0), z_right)
        wait(f"Fo{j}-", f"Fm{j}-")
        got[f"Ff{j}-"] = push(f_place(j, lax.rem(z + 1, 4), 1), f_place(j, lax.rem(z + 1, 4), 1), z_left)

    def do_fd(j):
        wait(f"Ff{j}+", f"Ff{j}-")
        f_high[j], f_low[j] = split(f_all[j])

    across, right, left = lax.rem(y + 2, 4), lax.rem(y + 1, 4), lax.rem(y + 3, 4)

    def sum_far(name, j, part, far, half):
        upper, lower = pl.ds(0, half), pl.ds(half, half)
        got[f"{name}{j}f+"] = push(part.at[j, across, upper], far.at[j, 0], y_right)
        got[f"{name}{j}f-"] = push(part.at[j, across, lower], far.at[j, 1], y_left)

    def sum_near(name, j, part, near, half):
        upper, lower = pl.ds(0, half), pl.ds(half, half)
        got[f"{name}{j}n+"] = push(part.at[j, right, lower], near.at[j, 0, lower], y_right)
        got[f"{name}{j}n-"] = push(part.at[j, left, upper], near.at[j, 1, upper], y_left)

    def sum_add(name, j, part, far, near, half):
        upper, lower = pl.ds(0, half), pl.ds(half, half)
        wait(f"{name}{j}f+")
        part[j, right, upper] = part[j, right, upper] + far[j, 0]
        got[f"{name}{j}a+"] = push(part.at[j, right, upper], near.at[j, 0, upper], y_right)
        wait(f"{name}{j}f-")
        part[j, left, lower] = part[j, left, lower] + far[j, 1]
        got[f"{name}{j}a-"] = push(part.at[j, left, lower], near.at[j, 1, lower], y_left)

    def total(name, j, part, near):
        wait(f"{name}{j}n+", f"{name}{j}n-", f"{name}{j}a+", f"{name}{j}a-")
        return part[j, y] + near[j, 0] + near[j, 1]

    def product1(j, blocks):
        for block in blocks:
            p1[j, block] = dot3(a_high[block], a_low[block], f_high[j], f_low[j])

    def do_m1(j):
        product1(j, (across,))
        sum_far("R1", j, p1, far1, u)

    def do_m1r(j):
        product1(j, (right, left, y))
        sum_near("R1", j, p1, near1, u)

    def do_r1a(j):
        sum_add("R1", j, p1, far1, near1, u)

    z_first = fresh(2 * CHUNKS)
    z_send = fresh(2 * CHUNKS)
    g_first = fresh(2 * CHUNKS)
    g_send = fresh(2 * CHUNKS)
    moves = []

    def place_out(src, dst, lane, send, recv):
        here = jnp.logical_and(jnp.logical_and(l == h, k == h), l == lane)
        copy = remote(src, dst, at(x, y, 2 * l + lane, h), send, recv)
        local = pltpu.make_async_copy(src, dst, recv_sems.at[recv])

        @pl.when(here)
        def _():
            local.start()

        @pl.when(jnp.logical_not(here))
        def _():
            copy.start()

        moves.append((here, copy))

    def z_place(j, xx, zz):
        position = lax.rem(zz, 2) * 2 + lax.div(zz, 2)
        return z_all.at[j, lax.rem(xx, 4), :, pl.ds(mult(position * rows, rows), rows)]

    def z_turned(j, zz):
        return z_turn.at[j, lax.rem(zz, 2) * 2 + lax.div(zz, 2)]

    def do_t1(j):
        value = -total("R1", j, p1, near1)
        z_own[j] = value
        turned = jnp.transpose(value)
        for piece in range(4):
            z_turn[j, piece] = turned[piece * w : (piece + 1) * w]
        z_place(j, x, z)[...] = z_turned(j, z)[...]
        for name, d in (("2", 2), ("+", 1), ("-", 3)):
            got[f"Zs{j}{name}"] = push(z_turned(j, lax.rem(z + d, 4)), z_place(j, x, z), at(x, y, z + d, k))
        mine = f_all[j, pl.ds(mult((l * 2 + h) * rows, rows), rows)]
        c_part[pl.ds(j, 1)] = c_part[pl.ds(j, 1)] - jnp.sum(value * mine, axis=0, keepdims=True)

    def do_zo(j):
        for lane in range(2):
            place_out(
                z_own.at[j, :, pl.ds(lane * u, u)],
                z_stage.at[k, j],
                lane,
                z_send + j * 2 + lane,
                z_first + k * CHUNKS + j,
            )

    def z_half(j, xx, half):
        return z_all.at[j, lax.rem(xx, 4), :, pl.ds(half * 4 * u, 4 * u)]

    def do_zn(j):
        wait(f"Zs{j}2", f"Zs{j}+", f"Zs{j}-")
        for half in range(2):
            ring_half(f"Zn{j}{half}", z_half(j, x, half), x_right, x_left)

    def do_zf(j):
        wait(f"Zn{j}0+")
        got[f"Zf{j}+"] = push(z_half(j, x + 3, 0), z_half(j, x + 3, 0), x_right)
        wait(f"Zn{j}1-")
        got[f"Zf{j}-"] = push(z_half(j, x + 1, 1), z_half(j, x + 1, 1), x_left)

    def do_zd(j):
        wait(f"Zn{j}1+", f"Zn{j}0-", f"Zf{j}+", f"Zf{j}-")
        for xx in range(4):
            zh[j, pl.ds(xx * w, w)], zl[j, pl.ds(xx * w, w)] = split(z_all[j, xx])

    def do_m2(j):
        for q in range(CHUNKS):
            value = dot3(zh[j], zl[j], f_high[q], f_low[q])
            for block in range(4):
                for lane in range(2):
                    p2[j, block, :, pl.ds((lane * CHUNKS + q) * u, u)] = value[
                        block * w : (block + 1) * w, lane * u : (lane + 1) * u
                    ]
        sum_far("R2", j, p2, far2, w // 2)

    def do_m2r(j):
        sum_near("R2", j, p2, near2, w // 2)

    def do_r2a(j):
        sum_add("R2", j, p2, far2, near2, w // 2)

    def do_t2(j):
        g_own[j] = total("R2", j, p2, near2)
        for lane in range(2):
            place_out(
                g_own.at[j, :, pl.ds(lane * 4 * u, 4 * u)],
                g_stage.at[k, pl.ds(j * w, w)],
                lane,
                g_send + j * 2 + lane,
                g_first + k * CHUNKS + j,
            )

    def prepare_diagonals():
        eye = lax.broadcasted_iota(jnp.int32, (rows, rows), 0) == lax.broadcasted_iota(jnp.int32, (rows, rows), 1)

        def diagonal(tile):
            return jnp.sum(jnp.where(eye, tile, 0.0), axis=0, keepdims=True)

        dd_send[...] = jnp.zeros_like(dd_send)
        dd_send[0, pl.ds(0, 1)] = diagonal(anc_ref[:, own_lanes])
        dd_send[1, pl.ds(0, 1)] = diagonal(diag_ref[other, :, own_lanes])
        dd_send[2, pl.ds(0, 1)] = diagonal(diag_ref[k, :, own_lanes])
        got["Da"] = push(dd_send.at[0], dd_recv.at[0], z_mate)
        got["Dd"] = push(dd_send.at[1], dd_recv.at[1], sibling)

    def start_sums():
        wait("Da", "Dd")
        zd[...] = jnp.where(l == h, dd_send[0], dd_recv[0])
        scale = jnp.logical_and(x == y, l == h).astype(f32)
        mine = dd_send[2, pl.ds(0, 1)]
        theirs = dd_recv[1, pl.ds(0, 1)]
        first = jnp.where(k == 0, mine, theirs) * scale
        last = jnp.where(k == 0, theirs, mine) * scale
        c_part[...] = jnp.zeros_like(c_part)
        for pair in range(2):
            woven = weave(first[:, pair * u : (pair + 1) * u], last[:, pair * u : (pair + 1) * u])
            for i in range(2):
                for lane in range(2):
                    c_part[pl.ds(2 * pair + i, 1), pl.ds(lane * u, u)] = woven[i] * (l == lane).astype(f32)

    def do_ca():
        for d in (1, 2, 3):
            got[f"Ca{d}"] = push(c_part, c_plane.at[d - 1], at(x, y, z + d, k))

    def do_cb():
        wait("Ca1", "Ca2", "Ca3")
        c_line[0] = c_part[...] + c_plane[0] + (c_plane[1] + c_plane[2])
        for d in (1, 2, 3):
            got[f"Cb{d}"] = push(c_line.at[0], c_line.at[d], at(x, y + d, z, k))

    def do_cc():
        wait("Cb1", "Cb2", "Cb3")
        c_front[...] = c_line[0] + c_line[1] + (c_line[2] + c_line[3])
        c_all[x, k] = c_front[...]
        got["Cc"] = push(c_front, c_all.at[x, k], sibling)

    def do_cd():
        wait("Cc")
        c_all[x, 2] = zd[...]
        for d in (1, 2, 3):
            got[f"Cd{d}"] = push(c_all.at[x], c_all.at[x], at(x + d, y, z, k))

    def columns(xx, front, lane):
        blocks = [c_all[xx, front, pl.ds(q, 1), pl.ds(mult(lane * u, u), u)] for q in range(CHUNKS)]
        woven = [weave(blocks[2 * pair], blocks[2 * pair + 1]) for pair in range(2)]
        return jnp.concatenate([woven[0][0], woven[1][0]], axis=1), jnp.concatenate([woven[0][1], woven[1][1]], axis=1)

    def prepare_edges():
        for front in range(2):
            step = lax.broadcasted_iota(jnp.int32, (4 * u, near_ref.shape[1]), 0)
            hot_near[front] = (step == near_ref[pl.ds(front, 1), :]).astype(f32).astype(jnp.bfloat16)
            hot_far[front] = (step == far_ref[pl.ds(front, 1), :]).astype(f32)

    def do_ce():
        wait("Cd1", "Cd2", "Cd3")
        for front in range(2):
            table[...] = jnp.zeros_like(table)
            first, last = columns(x, front, l)
            table[pl.ds(0, 1), pl.ds(0, rows)] = first
            table[pl.ds(0, 1), pl.ds(rows, rows)] = last
            near = pick(table[...], hot_near[front])
            first, last = columns(y, front, h)
            table[pl.ds(0, 1), pl.ds(0, rows)] = jnp.where(k == 0, first, last)
            table[pl.ds(0, 1), pl.ds(rows, rows)] = c_all[y, 2, pl.ds(0, 1)]
            far = pick(table[...], hot_far[front].astype(jnp.bfloat16))
            r_part[pl.ds(front, 1)] = near[0:1] + far[0:1]

    def arrived(here, sem):
        pltpu.make_async_copy(here, here, recv_sems.at[sem]).wait()

    def finish_z():
        for front in range(2):
            for j in range(CHUNKS):
                arrived(z_stage.at[front, j], z_first + front * CHUNKS + j)
            for pair in range(2):
                woven = weave(z_stage[front, 2 * pair], z_stage[front, 2 * pair + 1])
                for i in range(2):
                    z_out[front, :, pl.ds((2 * i + pair) * u, u)] = woven[i]
            chosen = pick(z_out[front], hot_near[front]) * hot_far[front, pl.ds(rows, rows)]
            r_part[pl.ds(front, 1)] = r_part[pl.ds(front, 1)] - 2.0 * jnp.sum(chosen, axis=0, keepdims=True)

    def finish_g():
        for front in range(2):
            for j in range(CHUNKS):
                arrived(g_stage.at[front, pl.ds(j * w, w)], g_first + front * CHUNKS + j)
            for pair in range(2):
                woven = weave(
                    g_stage[front, :, pl.ds(2 * pair * u, u)], g_stage[front, :, pl.ds((2 * pair + 1) * u, u)]
                )
                for i in range(2):
                    lanes = pl.ds((2 * i + pair) * u, u)
                    g_out[front, :, lanes] = diag_ref[front, :, lanes] - woven[i]
            chosen = pick(g_out[front], hot_near[front]) * hot_far[front, pl.ds(0, rows)]
            r_out[pl.ds(front, 1)] = r_part[pl.ds(front, 1)] - 2.0 * jnp.sum(chosen, axis=0, keepdims=True)

    steps = {
        "Ap": do_ap, "Ao": do_ao, "Am": do_am, "Af": do_af, "At": do_at, "Ad": do_ad,
        "Fp": do_fp, "Fo": do_fo, "Fm": do_fm, "Ff": do_ff, "Fd": do_fd,
        "M1": do_m1, "M1r": do_m1r, "R1a": do_r1a, "T1": do_t1,
        "Zo": do_zo, "Zn": do_zn, "Zf": do_zf, "Zd": do_zd,
        "M2": do_m2, "M2r": do_m2r, "R2a": do_r2a, "T2": do_t2,
        "Ds": start_sums, "Ed": prepare_edges, "Ca": do_ca, "Cb": do_cb, "Cc": do_cc, "Cd": do_cd, "Ce": do_ce,
    }
    pl.semaphore_wait(barrier, len(greet))
    masked = False
    for step in ORDER:
        if step in steps:
            steps[step]()
        else:
            if not masked:
                mask_factor()
                prepare_diagonals()
                masked = True
            steps[step[:-1]](int(step[-1]))
    finish_z()
    finish_g()

    for here, copy in moves:

        @pl.when(jnp.logical_not(here))
        def _():
            copy.wait_send()

    for copy in sent:
        copy.wait_send()


def per_device(anc_inverse, off_factor, diag_inverse, block_mask, edge_child, edge_other):
    fronts, rows, width = off_factor.shape
    edges = edge_child.shape[1]
    u = rows // 2
    w = u // 2
    n = CHUNKS
    f32, bf16 = jnp.float32, jnp.bfloat16
    vmem = pl.BlockSpec(memory_space=pltpu.VMEM)
    scratch = [
        ((n, rows, u), f32),
        ((n, 8 * u, 2 * u), f32),
        ((n, 8 * u, 2 * u), bf16),
        ((n, 8 * u, 2 * u), bf16),
        ((rows, rows), f32),
        ((4, rows, 8 * u), f32),
        ((4, rows, 8 * u), bf16),
        ((4, rows, 8 * u), bf16),
        ((n, 4, rows, 2 * u), f32),
        ((n, 2, u, 2 * u), f32),
        ((n, 2, rows, 2 * u), f32),
        ((n, rows, 2 * u), f32),
        ((n, 4, w, rows), f32),
        ((n, 4, w, 8 * u), f32),
        ((n, 4 * w, 8 * u), bf16),
        ((n, 4 * w, 8 * u), bf16),
        ((2, n, rows, u), f32),
        ((n, 4, w, 8 * u), f32),
        ((n, 2, w // 2, 8 * u), f32),
        ((n, 2, w, 8 * u), f32),
        ((n, w, 8 * u), f32),
        ((2, rows, 4 * u), f32),
        ((3, 8, rows), f32),
        ((2, 8, rows), f32),
        ((8, rows), f32),
        ((3, 8, rows), f32),
        ((4, 8, rows), f32),
        ((8, rows), f32),
        ((4, 3, 8, rows), f32),
        ((8, rows), f32),
        ((8, 4 * u), f32),
        ((2, 4 * u, edges), bf16),
        ((2, 4 * u, edges), f32),
        ((8, edges), f32),
    ]
    supercols = width * lax.axis_size("col")
    row_start = lax.axis_index("row") * rows
    near_at = edge_child - lax.axis_index("col") * width
    far_at = edge_other - row_start
    far_at = jnp.where(edge_other < supercols, far_at, far_at - supercols + rows)
    flops = 2 * 3 * 2 * (8 * u) ** 3
    return pl.pallas_call(
        functools.partial(kernel, u),
        out_shape=(
            jax.ShapeDtypeStruct(off_factor.shape, f32),
            jax.ShapeDtypeStruct(diag_inverse.shape, f32),
            jax.ShapeDtypeStruct((fronts, edges), f32),
        ),
        in_specs=[pl.BlockSpec(memory_space=pltpu.SMEM)] + [vmem] * 5,
        out_specs=(vmem, vmem, vmem),
        scratch_shapes=[pltpu.VMEM(*entry) for entry in scratch]
        + [pltpu.SemaphoreType.DMA((SEMAPHORES,)), pltpu.SemaphoreType.DMA((SEMAPHORES,))],
        compiler_params=pltpu.CompilerParams(collective_id=0, has_side_effects=True, vmem_limit_bytes=60 << 20),
        cost_estimate=pl.CostEstimate(flops=flops, bytes_accessed=5 << 20, transcendentals=0),
    )(block_mask, anc_inverse, off_factor, diag_inverse, near_at, far_at)


def solution(mesh):
    placed = (
        P("row", "col"),
        P(None, "row", "col"),
        P(None, "row", "col"),
        P(None, "row"),
        P(None, ("row", "col")),
        P(None, ("row", "col")),
    )
    return jax.shard_map(
        per_device,
        mesh=mesh,
        in_specs=placed,
        out_specs=(P(None, "row", "col"), P(None, "row", "col"), P(None, ("row", "col"))),
        check_vma=False,
    )
```

```python
import functools

import jax
import jax.numpy as jnp
from jax import lax
from jax.experimental import pallas as pl
from jax.experimental.pallas import tpu as pltpu
from jax.sharding import PartitionSpec as P

MESH = pl.DeviceIdType.MESH
CHUNKS = 4
SEMAPHORES = 384
BOTH_WAYS = (0, 1, 2, 3)

ORDER = (
    "Ap1", "Ao1", "Ap0", "Am1", "Fp2", "Fo1", "Fp1", "Ar1", "Fm1", "Ao0", "Ed", "Al1", "Am0", "Fo2", "Aq1", "Ff1", "Da", "Ar0", "At1", "Al0",
    "Fp0", "Fm2", "Aq0", "Ad1", "Fd1", "M13", "Fo0", "M1r3", "At0", "Ff2", "R1a3", "Ad0", "M12", "Fp3", "Ds", "M1r2", "Fm0", "R1a2", "Fo3",
    "Fd2", "M14", "M15", "M1r4", "Ff0", "M1r5", "R1a5", "Fm3", "R1a4", "Fd0", "M10", "T12", "M11", "T13", "M1r1", "Ff3", "M1r0", "R1a0",
    "R1a1", "Zn3", "T15", "T14", "Fd3", "Zn2", "M16", "M17", "M1r7", "Zf3", "M1r6", "T11", "Zn5", "R1a6", "Zo2", "T10", "R1a7", "Zd3", "Zf2",
    "M23", "Zn4", "Zd2", "M22", "Zf5", "Zf4", "T16", "R2a3", "Zn0", "Zd5", "M25", "Zd4", "Zn1", "R2a2", "T17", "Ca", "Zo1", "Zf0", "M24",
    "R2a5", "Zf1", "Zn6", "T22", "Zd0", "Zo0", "M20", "R2a4", "Cb", "Zn7", "Zd1", "M21", "Zf6", "Zf7", "R2a0", "Zd6", "Zo3", "M26", "Zd7",
    "T25", "Cc", "T24", "R2a1", "Cd", "T20", "M27", "T23", "Ce", "T21", "R2a6", "R2a7", "T26", "T27", "Ez",
)


def place():
    row = lax.axis_index("row")
    col = lax.axis_index("col")
    return lax.div(col, 2), lax.div(row, 4), lax.rem(lax.div(row, 2), 2), lax.rem(col, 2), lax.rem(row, 2)


def at(x, y, z, k):
    x, y, z, k = lax.rem(x, 4), lax.rem(y, 4), lax.rem(z, 4), lax.rem(k, 2)
    return (y * 4 + lax.div(z, 2) * 2 + k, x * 2 + lax.rem(z, 2))


def split(value):
    high = value.astype(jnp.bfloat16)
    return high, (value - high.astype(jnp.float32)).astype(jnp.bfloat16)


def dot3(left_high, left_low, right_high, right_low):
    def dot(left, right):
        return jnp.dot(left, right, preferred_element_type=jnp.float32)

    return dot(left_high, right_high) + (dot(left_high, right_low) + dot(left_low, right_high))


def pick(value, hot):
    high, rest = split(value)
    low = value - high.astype(jnp.float32) - rest.astype(jnp.float32)
    parts = (high, rest, low.astype(jnp.bfloat16))
    return sum(jnp.dot(part, hot, preferred_element_type=jnp.float32) for part in parts)


def weave(first, second):
    half = first.shape[1] // 2
    low = lax.broadcasted_iota(jnp.int32, first.shape, 1) < half
    return (
        jnp.where(low, first, pltpu.roll(second, half, 1)),
        jnp.where(low, pltpu.roll(first, half, 1), second),
    )


def one_hot(u, near_ref, far_ref, hot_near, hot_far):
    rows = 2 * u
    for front in range(2):
        step = lax.broadcasted_iota(jnp.int32, (4 * u, near_ref.shape[1]), 0)
        near = near_ref[pl.ds(front, 1), :] - lax.axis_index("col") * 4 * u
        far = far_ref[pl.ds(front, 1), :]
        start = lax.axis_index("row") * rows
        far = jnp.where(far < 32 * u, far - start, far - 32 * u - start + rows)
        hot_near[front] = (step == near).astype(jnp.float32).astype(jnp.bfloat16)
        hot_far[front] = (step == far).astype(jnp.float32)


def finish(u, z_ref, g_ref, diag_ref, r_ref, z_out, g_out, r_out):
    r_out[...] = r_ref[0:2]
    z_out[...] = z_ref[...]
    for front in range(2):
        for pair in range(2):
            woven = weave(
                g_ref[front, :, pl.ds(2 * pair * u, u)], g_ref[front, :, pl.ds((2 * pair + 1) * u, u)]
            )
            for i in range(2):
                lanes = pl.ds((2 * i + pair) * u, u)
                g_out[front, :, lanes] = diag_ref[front, :, lanes] - woven[i]


def kernel(
    u,
    mask_ref,
    anc_ref,
    fac_ref,
    diag_ref,
    near_ref,
    far_ref,
    z_out,
    g_stage,
    r_part,
    f_send,
    f_all,
    f_high,
    f_low,
    a_turn,
    a_all,
    a_high,
    a_low,
    p1,
    far1,
    near1,
    z_own,
    z_turn,
    z_all,
    zh,
    zl,
    z_stage,
    p2,
    far2,
    near2,
    g_own,
    dd_send,
    dd_recv,
    c_part,
    c_plane,
    c_line,
    c_front,
    c_all,
    zd,
    table,
    hot_near,
    hot_far,
    hot_stage,
    send_sems,
    recv_sems,
):
    x, y, h, l, k = place()
    z = 2 * h + l
    rows = 2 * u
    w = u // 2
    f32 = jnp.float32
    other = 1 - k

    count = [0]

    def fresh(n=1):
        first = count[0]
        count[0] += n
        return first

    def mult(value, of):
        return pl.multiple_of(value, of)

    def remote(src, dst, device, send, recv):
        return pltpu.make_async_remote_copy(
            src_ref=src,
            dst_ref=dst,
            send_sem=send_sems.at[send],
            recv_sem=recv_sems.at[recv],
            device_id=device,
            device_id_type=MESH,
        )

    sent = []

    def push(src, dst, device):
        i = fresh()
        copy = remote(src, dst, device, i, i)
        copy.start()
        sent.append(copy)
        return copy

    sibling = at(x, y, z, k + 1)
    x_right, x_left = at(x + 1, y, z, k), at(x + 3, y, z, k)
    y_right, y_left = at(x, y + 1, z, k), at(x, y + 3, z, k)
    mate, outer = 2 * h + 1 - l, lax.rem(z + 3 + 2 * l, 4)
    z_mate, z_outer, z_across = at(x, y, mate, k), at(x, y, outer, k), at(x, y, z + 2, k)

    barrier = pltpu.get_barrier_semaphore()
    greet = (z_across, z_outer, z_mate, sibling, x_right, x_left, y_right, y_left)
    for device in greet:
        pl.semaphore_signal(barrier, inc=1, device_id=device, device_id_type=MESH)

    own_lanes = pl.ds(mult(k * rows, rows), rows)

    def a_place(xx, hh, kk, a):
        lanes = pl.ds(mult((hh * 2 + kk) * rows, rows), rows)
        return a_all.at[lax.rem(xx, 4), pl.ds(a * u, u), lanes]

    def turn_ancestor():
        for half in range(2):
            a_turn[half] = jnp.transpose(anc_ref[:, half * rows : (half + 1) * rows])

    def f_place(j, zz, half):
        row = (lax.div(zz, 2) * 2 + half) * rows
        return f_all.at[j, pl.ds(mult(row, rows), rows), pl.ds(mult(lax.rem(zz, 2) * u, u), u)]

    def mask_factor():
        for front, mine in ((other, False), (k, True)):
            for b in range(2):
                source = pl.ds(b * u, u)
                keep = mask_ref[front, b].astype(f32)
                for pair in range(2):
                    woven = weave(
                        fac_ref[front, source, pl.ds(pair * u, u)] * keep,
                        fac_ref[front, source, pl.ds((2 + pair) * u, u)] * keep,
                    )
                    for i in range(2):
                        if mine:
                            f_place(2 * pair + i, z, k).at[source][...] = woven[i]
                        else:
                            f_send[2 * pair + i, source] = woven[i]

    got = {}
    waited = set()

    def ring_half(name, src, right, left):
        got[name + "+"] = push(src, src, right)
        got[name + "-"] = push(src, src, left)

    def wait(*names):
        for name in names:
            if name not in waited:
                waited.add(name)
                got[name].wait_recv()

    a_first = fresh(4)
    a_sends = fresh(4)
    moves = []

    def move(here, src, dst, device, send, recv):
        copy = remote(src, dst, device, send, recv)
        local = pltpu.make_async_copy(src, dst, recv_sems.at[recv])

        @pl.when(here)
        def _():
            local.start()

        @pl.when(jnp.logical_not(here))
        def _():
            copy.start()

        moves.append((here, copy))

    def arrived(here, sem):
        pltpu.make_async_copy(here, here, recv_sems.at[sem]).wait()

    def to_sibling(a, i, xx, hh):
        got[f"As{a}{i}"] = push(a_place(xx, hh, k, a), a_place(xx, hh, k, a), sibling)

    def do_ap(a):
        for half in range(2):
            here = jnp.logical_and(l == h, l == half)
            move(
                here,
                a_turn.at[half, pl.ds(a * u, u)],
                a_place(x, h, k, a),
                at(x, y, 2 * l + half, k),
                a_sends + a * 2 + half,
                a_first + a * 2 + h,
            )

    def do_ao(a):
        arrived(a_place(x, h, k, a), a_first + a * 2 + h)
        ring_half(f"Ao{a}", a_place(x, h, k, a), x_right, x_left)
        to_sibling(a, 0, x, h)

    def do_am(a):
        arrived(a_place(x, 1 - h, k, a), a_first + a * 2 + 1 - h)
        ring_half(f"Am{a}", a_place(x, 1 - h, k, a), x_right, x_left)
        to_sibling(a, 1, x, 1 - h)

    def do_ar(a):
        wait(f"Ao{a}+")
        got[f"Af{a}+"] = push(a_place(x + 3, h, k, a), a_place(x + 3, h, k, a), x_right)
        to_sibling(a, 2, x + 3, h)

    def do_al(a):
        wait(f"Am{a}-")
        got[f"Af{a}-"] = push(a_place(x + 1, 1 - h, k, a), a_place(x + 1, 1 - h, k, a), x_left)
        to_sibling(a, 3, x + 1, 1 - h)

    def do_aq(a):
        wait(f"Ao{a}-", f"Am{a}+")
        to_sibling(a, 4, x + 1, h)
        to_sibling(a, 5, x + 3, 1 - h)

    def do_at(a):
        wait(f"Af{a}+", f"Af{a}-")
        for hh in range(2):
            to_sibling(a, 6 + hh, x + 2, hh)

    def do_ad(a):
        for i in range(8):
            wait(f"As{a}{i}")
        part = pl.ds(a * u, u)
        for xx in range(4):
            a_high[xx, part], a_low[xx, part] = split(a_all[xx, part])

    def do_fp(j):
        got[f"Fp{j}"] = push(f_send.at[j], f_place(j, z, k), sibling)

    def to_both(name, src):
        got[name + "m"] = push(src, src, z_mate)
        got[name + "o"] = push(src, src, z_outer)

    def do_fo(j):
        to_both(f"Fo{j}", f_place(j, z, k))

    def do_fm(j):
        wait(f"Fp{j}")
        to_both(f"Fm{j}", f_place(j, z, other))

    def f_block(j, zz):
        row = lax.div(zz, 2) * 2 * rows
        return f_all.at[j, pl.ds(mult(row, rows), 2 * rows), pl.ds(mult(lax.rem(zz, 2) * u, u), u)]

    def do_ff(j):
        wait(f"Fo{j}m", f"Fm{j}m")
        if j in BOTH_WAYS:
            got[f"Ff{j}+"] = push(f_place(j, mate, 0), f_place(j, mate, 0), z_outer)
            wait(f"Fo{j}o", f"Fm{j}o")
            got[f"Ff{j}-"] = push(f_place(j, outer, 1), f_place(j, outer, 1), z_mate)
        else:
            got[f"Ff{j}+"] = push(f_block(j, mate), f_block(j, mate), z_outer)

    def do_fd(j):
        wait(f"Ff{j}+", f"Ff{j}-" if j in BOTH_WAYS else f"Ff{j}+", f"Fo{j}o", f"Fm{j}o")
        f_high[j], f_low[j] = split(f_all[j])

    across, right, left = lax.rem(y + 2, 4), lax.rem(y + 1, 4), lax.rem(y + 3, 4)

    def sum_far(name, j, part, far, half):
        upper, lower = pl.ds(0, half), pl.ds(half, half)
        got[f"{name}{j}f+"] = push(part.at[j, across, upper], far.at[j, 0], y_right)
        got[f"{name}{j}f-"] = push(part.at[j, across, lower], far.at[j, 1], y_left)

    def sum_near(name, j, part, near, half):
        upper, lower = pl.ds(0, half), pl.ds(half, half)
        got[f"{name}{j}n+"] = push(part.at[j, right, lower], near.at[j, 0, lower], y_right)
        got[f"{name}{j}n-"] = push(part.at[j, left, upper], near.at[j, 1, upper], y_left)

    def sum_add(name, j, part, far, near, half):
        upper, lower = pl.ds(0, half), pl.ds(half, half)
        wait(f"{name}{j}f+")
        part[j, right, upper] = part[j, right, upper] + far[j, 0]
        got[f"{name}{j}a+"] = push(part.at[j, right, upper], near.at[j, 0, upper], y_right)
        wait(f"{name}{j}f-")
        part[j, left, lower] = part[j, left, lower] + far[j, 1]
        got[f"{name}{j}a-"] = push(part.at[j, left, lower], near.at[j, 1, lower], y_left)

    def total(name, j, part, near):
        wait(f"{name}{j}n+", f"{name}{j}n-", f"{name}{j}a+", f"{name}{j}a-")
        return part[j, y] + near[j, 0] + near[j, 1]

    def product1(c, blocks):
        j, part = c // 2, pl.ds((c % 2) * u, u)
        for block in blocks:
            p1[c, block] = dot3(a_high[block, part], a_low[block, part], f_high[j], f_low[j])

    def do_m1(c):
        product1(c, (across,))
        sum_far("R1", c, p1, far1, w)

    def do_m1r(c):
        product1(c, (right, left, y))
        sum_near("R1", c, p1, near1, w)

    def do_r1a(c):
        sum_add("R1", c, p1, far1, near1, w)

    z_first = fresh(2 * CHUNKS)
    z_send = fresh(2 * CHUNKS)
    g_first = fresh(4 * CHUNKS)
    g_send = fresh(4 * CHUNKS)

    def place_out(src, dst, lane, send, recv):
        move(jnp.logical_and(k == l, l == lane), src, dst, at(x, y, 2 * h + lane, l), send, recv)

    def do_t1(c):
        j, a = c // 2, c % 2
        value = -total("R1", c, p1, near1)
        z_own[j, pl.ds(a * u, u)] = value
        turned = jnp.transpose(value)
        for piece in range(4):
            z_turn[c, piece] = turned[piece * w : (piece + 1) * w]
        spot = z_all.at[j, x, :, pl.ds(mult(z * rows + a * u, u), u)]
        spot[...] = z_turn[c, z]
        for name, d in (("2", lax.rem(z + 2, 4)), ("m", mate), ("o", outer)):
            got[f"Zs{c}{name}"] = push(z_turn.at[c, d], spot, at(x, y, d, k))
        mine = f_all[j, pl.ds(mult(z * rows + a * u, u), u)]
        c_part[pl.ds(j, 1)] = c_part[pl.ds(j, 1)] - jnp.sum(value * mine, axis=0, keepdims=True)

    def do_zo(j):
        for lane in range(2):
            place_out(
                z_own.at[j, :, pl.ds(lane * u, u)],
                z_stage.at[k, j],
                lane,
                z_send + j * 2 + lane,
                z_first + k * CHUNKS + j,
            )

    def z_half(c, xx, half):
        return z_all.at[c // 2, lax.rem(xx, 4), pl.ds((c % 2) * (w // 2), w // 2), pl.ds(half * 4 * u, 4 * u)]

    def do_zn(c):
        wait(*(f"Zs{c // 2 * 2 + a}{name}" for a in range(2) for name in "2mo"))
        for half in range(2):
            ring_half(f"Zn{c}{half}", z_half(c, x, half), x_right, x_left)

    def do_zf(c):
        wait(f"Zn{c}0+")
        got[f"Zf{c}+"] = push(z_half(c, x + 3, 0), z_half(c, x + 3, 0), x_right)
        wait(f"Zn{c}1-")
        got[f"Zf{c}-"] = push(z_half(c, x + 1, 1), z_half(c, x + 1, 1), x_left)

    def do_zd(c):
        wait(f"Zn{c}1+", f"Zn{c}0-", f"Zf{c}+", f"Zf{c}-")
        v = w // 2
        for xx in range(4):
            part = z_all[c // 2, xx, pl.ds((c % 2) * v, v)]
            zh[c, pl.ds(xx * v, v)], zl[c, pl.ds(xx * v, v)] = split(part)

    def do_m2(c):
        v = w // 2
        for q in range(CHUNKS):
            value = dot3(zh[c], zl[c], f_high[q], f_low[q])
            for block in range(4):
                for lane in range(2):
                    p2[c, block, :, pl.ds((lane * CHUNKS + q) * u, u)] = value[
                        block * v : (block + 1) * v, lane * u : (lane + 1) * u
                    ]
        sum_far("R2", c, p2, far2, v // 2)
        sum_near("R2", c, p2, near2, v // 2)

    def do_r2a(c):
        sum_add("R2", c, p2, far2, near2, w // 4)

    def do_t2(c):
        g_own[c] = total("R2", c, p2, near2)
        for lane in range(2):
            place_out(
                g_own.at[c, :, pl.ds(lane * 4 * u, 4 * u)],
                g_stage.at[k, pl.ds(c * (w // 2), w // 2)],
                lane,
                g_send + c * 2 + lane,
                g_first + k * 2 * CHUNKS + c,
            )

    def prepare_diagonals():
        eye = lax.broadcasted_iota(jnp.int32, (rows, rows), 0) == lax.broadcasted_iota(jnp.int32, (rows, rows), 1)

        def diagonal(tile):
            return jnp.sum(jnp.where(eye, tile, 0.0), axis=0, keepdims=True)

        dd_send[...] = jnp.zeros_like(dd_send)
        dd_send[0, pl.ds(0, 1)] = diagonal(anc_ref[:, own_lanes])
        dd_send[1, pl.ds(0, 1)] = diagonal(diag_ref[other, :, own_lanes])
        dd_send[2, pl.ds(0, 1)] = diagonal(diag_ref[k, :, own_lanes])
        got["Da"] = push(dd_send.at[0], dd_recv.at[0], z_mate)
        got["Dd"] = push(dd_send.at[1], dd_recv.at[1], sibling)

    def start_sums():
        wait("Da", "Dd")
        zd[...] = jnp.where(l == h, dd_send[0], dd_recv[0])
        scale = jnp.logical_and(x == y, l == h).astype(f32)
        mine = dd_send[2, pl.ds(0, 1)]
        theirs = dd_recv[1, pl.ds(0, 1)]
        first = jnp.where(k == 0, mine, theirs) * scale
        last = jnp.where(k == 0, theirs, mine) * scale
        c_part[...] = jnp.zeros_like(c_part)
        for pair in range(2):
            woven = weave(first[:, pair * u : (pair + 1) * u], last[:, pair * u : (pair + 1) * u])
            for i in range(2):
                for lane in range(2):
                    c_part[pl.ds(2 * pair + i, 1), pl.ds(lane * u, u)] = woven[i] * (l == lane).astype(f32)

    def do_ca():
        for d in (1, 2, 3):
            got[f"Ca{d}"] = push(c_part, c_plane.at[d - 1], at(x, y, z + d, k))

    def do_cb():
        wait("Ca1", "Ca2", "Ca3")
        c_line[0] = c_part[...] + c_plane[0] + (c_plane[1] + c_plane[2])
        for d in (1, 2, 3):
            got[f"Cb{d}"] = push(c_line.at[0], c_line.at[d], at(x, y + d, z, k))

    def do_cc():
        wait("Cb1", "Cb2", "Cb3")
        c_front[...] = c_line[0] + c_line[1] + (c_line[2] + c_line[3])
        c_all[x, k] = c_front[...]
        got["Cc"] = push(c_front, c_all.at[x, k], sibling)

    def do_cd():
        wait("Cc")
        c_all[x, 2] = zd[...]
        for d in (1, 2, 3):
            got[f"Cd{d}"] = push(c_all.at[x], c_all.at[x], at(x + d, y, z, k))

    def columns(xx, front, lane):
        blocks = [c_all[xx, front, pl.ds(q, 1), pl.ds(mult(lane * u, u), u)] for q in range(CHUNKS)]
        woven = [weave(blocks[2 * pair], blocks[2 * pair + 1]) for pair in range(2)]
        return jnp.concatenate([woven[0][0], woven[1][0]], axis=1), jnp.concatenate([woven[0][1], woven[1][1]], axis=1)

    def prepare_edges():
        one_hot(u, near_ref, far_ref, hot_near, hot_far)
        bits = u.bit_length() - 1
        step = lax.broadcasted_iota(jnp.int32, (4 * u, near_ref.shape[1]), 0)
        column = ((step >> (bits - 1)) & 1) * 2 * u + (step >> bits) * w + (step & (w - 1))
        for front in range(2):
            near = near_ref[pl.ds(front, 1), :] - lax.axis_index("col") * 4 * u
            hot_stage[front] = (column == near).astype(f32).astype(jnp.bfloat16)

    def do_ce():
        wait("Cd1", "Cd2", "Cd3")
        for front in range(2):
            table[...] = jnp.zeros_like(table)
            first, last = columns(x, front, l)
            table[pl.ds(0, 1), pl.ds(0, rows)] = first
            table[pl.ds(0, 1), pl.ds(rows, rows)] = last
            near = pick(table[...], hot_near[front])
            first, last = columns(y, front, h)
            table[pl.ds(0, 1), pl.ds(0, rows)] = jnp.where(k == 0, first, last)
            table[pl.ds(0, 1), pl.ds(rows, rows)] = c_all[y, 2, pl.ds(0, 1)]
            far = pick(table[...], hot_far[front].astype(jnp.bfloat16))
            r_part[pl.ds(front, 1)] = near[0:1] + far[0:1]

    def finish_z():
        for front in range(2):
            for j in range(CHUNKS):
                arrived(z_stage.at[front, j], z_first + front * CHUNKS + j)
            for pair in range(2):
                woven = weave(z_stage[front, 2 * pair], z_stage[front, 2 * pair + 1])
                for i in range(2):
                    z_out[front, :, pl.ds((2 * i + pair) * u, u)] = woven[i]
            chosen = pick(z_out[front], hot_near[front]) * hot_far[front, pl.ds(rows, rows)]
            chosen = chosen + pick(diag_ref[front], hot_near[front]) * hot_far[front, pl.ds(0, rows)]
            r_part[pl.ds(front, 1)] = r_part[pl.ds(front, 1)] - 2.0 * jnp.sum(chosen, axis=0, keepdims=True)

    def finish_g():
        for front in range(2):
            for c in range(2 * CHUNKS):
                arrived(g_stage.at[front, pl.ds(c * (w // 2), w // 2)], g_first + front * 2 * CHUNKS + c)
            chosen = pick(g_stage[front], hot_stage[front]) * hot_far[front, pl.ds(0, rows)]
            r_part[pl.ds(front, 1)] = r_part[pl.ds(front, 1)] + 2.0 * jnp.sum(chosen, axis=0, keepdims=True)

    steps = {
        "Ap": do_ap, "Ao": do_ao, "Am": do_am, "Ar": do_ar, "Al": do_al, "Aq": do_aq, "At": do_at, "Ad": do_ad,
        "Fp": do_fp, "Fo": do_fo, "Fm": do_fm, "Ff": do_ff, "Fd": do_fd,
        "M1": do_m1, "M1r": do_m1r, "R1a": do_r1a, "T1": do_t1,
        "Zo": do_zo, "Zn": do_zn, "Zf": do_zf, "Zd": do_zd,
        "M2": do_m2, "R2a": do_r2a, "T2": do_t2, "Da": prepare_diagonals,
        "Ds": start_sums, "Ed": prepare_edges, "Ca": do_ca, "Cb": do_cb, "Cc": do_cc, "Cd": do_cd, "Ce": do_ce,
        "Ez": finish_z,
    }
    turn_ancestor()
    mask_factor()
    pl.semaphore_wait(barrier, len(greet))
    for step in ORDER:
        if step in steps:
            steps[step]()
        else:
            steps[step[:-1]](int(step[-1]))
    finish_g()

    for here, copy in moves:

        @pl.when(jnp.logical_not(here))
        def _():
            copy.wait_send()

    for copy in sent:
        copy.wait_send()


def per_device(anc_inverse, off_factor, diag_inverse, block_mask, edge_child, edge_other):
    fronts, rows, width = off_factor.shape
    edges = edge_child.shape[1]
    u = rows // 2
    w = u // 2
    n = CHUNKS
    f32, bf16 = jnp.float32, jnp.bfloat16
    vmem = pl.BlockSpec(memory_space=pltpu.VMEM)
    m, v = 2 * n, w // 2
    scratch = [
        ((n, rows, u), f32),
        ((n, 8 * u, 2 * u), f32),
        ((n, 8 * u, 2 * u), bf16),
        ((n, 8 * u, 2 * u), bf16),
        ((2, rows, rows), f32),
        ((4, rows, 8 * u), f32),
        ((4, rows, 8 * u), bf16),
        ((4, rows, 8 * u), bf16),
        ((m, 4, u, 2 * u), f32),
        ((m, 2, w, 2 * u), f32),
        ((m, 2, u, 2 * u), f32),
        ((n, rows, 2 * u), f32),
        ((m, 4, w, u), f32),
        ((n, 4, w, 8 * u), f32),
        ((m, 4 * v, 8 * u), bf16),
        ((m, 4 * v, 8 * u), bf16),
        ((2, n, rows, u), f32),
        ((m, 4, v, 8 * u), f32),
        ((m, 2, v // 2, 8 * u), f32),
        ((m, 2, v, 8 * u), f32),
        ((m, v, 8 * u), f32),
        ((3, 8, rows), f32),
        ((2, 8, rows), f32),
        ((8, rows), f32),
        ((3, 8, rows), f32),
        ((4, 8, rows), f32),
        ((8, rows), f32),
        ((4, 3, 8, rows), f32),
        ((8, rows), f32),
        ((8, 4 * u), f32),
        ((2, 4 * u, edges), bf16),
        ((2, 4 * u, edges), f32),
        ((2, 4 * u, edges), bf16),
    ]
    flops = 2 * 3 * 2 * (8 * u) ** 3
    wide = jax.ShapeDtypeStruct((fronts, rows, width), f32)
    off_inverse, correction, partial = pl.pallas_call(
        functools.partial(kernel, u),
        out_shape=(wide, wide, jax.ShapeDtypeStruct((8, edges), f32)),
        in_specs=[pl.BlockSpec(memory_space=pltpu.SMEM)] + [vmem] * 5,
        out_specs=(vmem, vmem, vmem),
        scratch_shapes=[pltpu.VMEM(*entry) for entry in scratch]
        + [pltpu.SemaphoreType.DMA((SEMAPHORES,)), pltpu.SemaphoreType.DMA((SEMAPHORES,))],
        compiler_params=pltpu.CompilerParams(collective_id=0, has_side_effects=True, vmem_limit_bytes=60 << 20),
        cost_estimate=pl.CostEstimate(flops=flops, bytes_accessed=5 << 20, transcendentals=0),
    )(block_mask, anc_inverse, off_factor, diag_inverse, edge_child, edge_other)
    steps = 4
    block = pl.BlockSpec((fronts, rows // steps, width), lambda i: (0, i, 0))
    edge = pl.BlockSpec((fronts, edges), lambda i: (0, 0))
    return pl.pallas_call(
        functools.partial(finish, u),
        out_shape=(wide, wide, jax.ShapeDtypeStruct((fronts, edges), f32)),
        grid=(steps,),
        in_specs=[block, block, block, pl.BlockSpec((8, edges), lambda i: (0, 0))],
        out_specs=(block, block, edge),
    )(off_inverse, correction, diag_inverse, partial)


def solution(mesh):
    placed = (
        P("row", "col"),
        P(None, "row", "col"),
        P(None, "row", "col"),
        P(None, "row"),
        P(None, ("row", "col")),
        P(None, ("row", "col")),
    )
    return jax.shard_map(
        per_device,
        mesh=mesh,
        in_specs=placed,
        out_specs=(P(None, "row", "col"), P(None, "row", "col"), P(None, ("row", "col"))),
        check_vma=False,
    )
```

```python
import functools

import jax
import jax.numpy as jnp
from jax import lax
from jax.experimental import pallas as pl
from jax.experimental.pallas import tpu as pltpu
from jax.sharding import PartitionSpec as P

MESH = pl.DeviceIdType.MESH
CHUNKS = 4
SEMAPHORES = 384
BOTH_WAYS = (0, 1, 2, 3)

ORDER = (
    "Ap1", "Ao1", "Ap0", "Am1", "Fp2", "Fo1", "Fp1", "Ar1", "Fm1", "Ao0", "Ed", "Al1", "Am0", "Fo2", "Aq1", "Ff1", "Da", "Ar0", "At1", "Al0",
    "Fp0", "Fm2", "Aq0", "Ad1", "Fd1", "M13", "Fo0", "M1r3", "At0", "Ff2", "R1a3", "Ad0", "M12", "Fp3", "Ds", "M1r2", "Fm0", "R1a2", "Fo3",
    "Fd2", "M14", "M15", "M1r4", "Ff0", "M1r5", "R1a5", "Fm3", "R1a4", "Fd0", "M10", "T12", "M11", "T13", "M1r1", "Ff3", "M1r0", "R1a0",
    "R1a1", "Zn3", "T15", "T14", "Fd3", "Zn2", "M16", "M17", "M1r7", "Zf3", "M1r6", "T11", "Zn5", "R1a6", "Zo2", "T10", "R1a7", "Zd3", "Zf2",
    "M23", "Zn4", "Zd2", "M22", "Zf5", "Zf4", "T16", "R2a3", "Zn0", "Zd5", "M25", "Zd4", "Zn1", "R2a2", "T17", "Ca", "Zo1", "Zf0", "M24",
    "R2a5", "Zf1", "Zn6", "T22", "Zd0", "Zo0", "M20", "R2a4", "Cb", "Zn7", "Zd1", "M21", "Zf6", "Zf7", "R2a0", "Zd6", "Zo3", "M26", "Zd7",
    "T25", "Cc", "T24", "R2a1", "Cd", "T20", "M27", "T23", "Ce", "T21", "R2a6", "R2a7", "T26", "T27", "Ez",
)


def place():
    row = lax.axis_index("row")
    col = lax.axis_index("col")
    return lax.div(col, 2), lax.div(row, 4), lax.rem(lax.div(row, 2), 2), lax.rem(col, 2), lax.rem(row, 2)


def at(x, y, z, k):
    x, y, z, k = lax.rem(x, 4), lax.rem(y, 4), lax.rem(z, 4), lax.rem(k, 2)
    return (y * 4 + lax.div(z, 2) * 2 + k, x * 2 + lax.rem(z, 2))


def split(value):
    high = value.astype(jnp.bfloat16)
    return high, (value - high.astype(jnp.float32)).astype(jnp.bfloat16)


def dot3(left_high, left_low, right_high, right_low):
    def dot(left, right):
        return jnp.dot(left, right, preferred_element_type=jnp.float32)

    return dot(left_high, right_high) + (dot(left_high, right_low) + dot(left_low, right_high))


def pick(value, hot):
    high, rest = split(value)
    low = value - high.astype(jnp.float32) - rest.astype(jnp.float32)
    parts = (high, rest, low.astype(jnp.bfloat16))
    return sum(jnp.dot(part, hot, preferred_element_type=jnp.float32) for part in parts)


def weave(first, second):
    half = first.shape[1] // 2
    low = lax.broadcasted_iota(jnp.int32, first.shape, 1) < half
    return (
        jnp.where(low, first, pltpu.roll(second, half, 1)),
        jnp.where(low, pltpu.roll(first, half, 1), second),
    )


def one_hot(u, near_ref, far_ref, hot_near, hot_far):
    rows = 2 * u
    for front in range(2):
        step = lax.broadcasted_iota(jnp.int32, (4 * u, near_ref.shape[1]), 0)
        near = near_ref[pl.ds(front, 1), :] - lax.axis_index("col") * 4 * u
        far = far_ref[pl.ds(front, 1), :]
        start = lax.axis_index("row") * rows
        far = jnp.where(far < 32 * u, far - start, far - 32 * u - start + rows)
        hot_near[front] = (step == near).astype(jnp.float32).astype(jnp.bfloat16)
        hot_far[front] = (step == far).astype(jnp.float32)


def kernel(
    u,
    mask_ref,
    anc_ref,
    fac_ref,
    diag_ref,
    near_ref,
    far_ref,
    z_out,
    g_out,
    r_out,
    f_send,
    f_all,
    f_high,
    f_low,
    a_turn,
    a_all,
    a_high,
    a_low,
    p1,
    far1,
    near1,
    z_own,
    z_turn,
    z_all,
    zh,
    zl,
    z_stage,
    p2,
    far2,
    near2,
    g_own,
    g_stage,
    dd_send,
    dd_recv,
    c_part,
    c_plane,
    c_line,
    c_front,
    c_all,
    zd,
    table,
    hot_near,
    hot_far,
    hot_stage,
    r_part,
    send_sems,
    recv_sems,
):
    x, y, h, l, k = place()
    z = 2 * h + l
    rows = 2 * u
    w = u // 2
    f32 = jnp.float32
    other = 1 - k

    count = [0]

    def fresh(n=1):
        first = count[0]
        count[0] += n
        return first

    def mult(value, of):
        return pl.multiple_of(value, of)

    def remote(src, dst, device, send, recv):
        return pltpu.make_async_remote_copy(
            src_ref=src,
            dst_ref=dst,
            send_sem=send_sems.at[send],
            recv_sem=recv_sems.at[recv],
            device_id=device,
            device_id_type=MESH,
        )

    sent = []

    def push(src, dst, device):
        i = fresh()
        copy = remote(src, dst, device, i, i)
        copy.start()
        sent.append(copy)
        return copy

    sibling = at(x, y, z, k + 1)
    x_right, x_left = at(x + 1, y, z, k), at(x + 3, y, z, k)
    y_right, y_left = at(x, y + 1, z, k), at(x, y + 3, z, k)
    mate, outer = 2 * h + 1 - l, lax.rem(z + 3 + 2 * l, 4)
    z_mate, z_outer, z_across = at(x, y, mate, k), at(x, y, outer, k), at(x, y, z + 2, k)

    barrier = pltpu.get_barrier_semaphore()
    greet = (z_across, z_outer, z_mate, sibling, x_right, x_left, y_right, y_left)
    for device in greet:
        pl.semaphore_signal(barrier, inc=1, device_id=device, device_id_type=MESH)

    own_lanes = pl.ds(mult(k * rows, rows), rows)

    def a_place(xx, hh, kk, a):
        lanes = pl.ds(mult((hh * 2 + kk) * rows, rows), rows)
        return a_all.at[lax.rem(xx, 4), pl.ds(a * u, u), lanes]

    def turn_ancestor():
        for half in range(2):
            a_turn[half] = jnp.transpose(anc_ref[:, half * rows : (half + 1) * rows])

    def f_place(j, zz, half):
        row = (lax.div(zz, 2) * 2 + half) * rows
        return f_all.at[j, pl.ds(mult(row, rows), rows), pl.ds(mult(lax.rem(zz, 2) * u, u), u)]

    def mask_factor():
        for front, mine in ((other, False), (k, True)):
            for b in range(2):
                source = pl.ds(b * u, u)
                keep = mask_ref[front, b].astype(f32)
                for pair in range(2):
                    woven = weave(
                        fac_ref[front, source, pl.ds(pair * u, u)] * keep,
                        fac_ref[front, source, pl.ds((2 + pair) * u, u)] * keep,
                    )
                    for i in range(2):
                        if mine:
                            f_place(2 * pair + i, z, k).at[source][...] = woven[i]
                        else:
                            f_send[2 * pair + i, source] = woven[i]

    got = {}
    waited = set()

    def ring_half(name, src, right, left):
        got[name + "+"] = push(src, src, right)
        got[name + "-"] = push(src, src, left)

    def wait(*names):
        for name in names:
            if name not in waited:
                waited.add(name)
                got[name].wait_recv()

    a_first = fresh(4)
    a_sends = fresh(4)
    moves = []

    def move(here, src, dst, device, send, recv):
        copy = remote(src, dst, device, send, recv)
        local = pltpu.make_async_copy(src, dst, recv_sems.at[recv])

        @pl.when(here)
        def _():
            local.start()

        @pl.when(jnp.logical_not(here))
        def _():
            copy.start()

        moves.append((here, copy))

    def arrived(here, sem):
        pltpu.make_async_copy(here, here, recv_sems.at[sem]).wait()

    def to_sibling(a, i, xx, hh):
        got[f"As{a}{i}"] = push(a_place(xx, hh, k, a), a_place(xx, hh, k, a), sibling)

    def do_ap(a):
        for half in range(2):
            here = jnp.logical_and(l == h, l == half)
            move(
                here,
                a_turn.at[half, pl.ds(a * u, u)],
                a_place(x, h, k, a),
                at(x, y, 2 * l + half, k),
                a_sends + a * 2 + half,
                a_first + a * 2 + h,
            )

    def do_ao(a):
        arrived(a_place(x, h, k, a), a_first + a * 2 + h)
        ring_half(f"Ao{a}", a_place(x, h, k, a), x_right, x_left)
        to_sibling(a, 0, x, h)

    def do_am(a):
        arrived(a_place(x, 1 - h, k, a), a_first + a * 2 + 1 - h)
        ring_half(f"Am{a}", a_place(x, 1 - h, k, a), x_right, x_left)
        to_sibling(a, 1, x, 1 - h)

    def do_ar(a):
        wait(f"Ao{a}+")
        got[f"Af{a}+"] = push(a_place(x + 3, h, k, a), a_place(x + 3, h, k, a), x_right)
        to_sibling(a, 2, x + 3, h)

    def do_al(a):
        wait(f"Am{a}-")
        got[f"Af{a}-"] = push(a_place(x + 1, 1 - h, k, a), a_place(x + 1, 1 - h, k, a), x_left)
        to_sibling(a, 3, x + 1, 1 - h)

    def do_aq(a):
        wait(f"Ao{a}-", f"Am{a}+")
        to_sibling(a, 4, x + 1, h)
        to_sibling(a, 5, x + 3, 1 - h)

    def do_at(a):
        wait(f"Af{a}+", f"Af{a}-")
        for hh in range(2):
            to_sibling(a, 6 + hh, x + 2, hh)

    def do_ad(a):
        for i in range(8):
            wait(f"As{a}{i}")
        part = pl.ds(a * u, u)
        for xx in range(4):
            a_high[xx, part], a_low[xx, part] = split(a_all[xx, part])

    def do_fp(j):
        got[f"Fp{j}"] = push(f_send.at[j], f_place(j, z, k), sibling)

    def to_both(name, src):
        got[name + "m"] = push(src, src, z_mate)
        got[name + "o"] = push(src, src, z_outer)

    def do_fo(j):
        to_both(f"Fo{j}", f_place(j, z, k))

    def do_fm(j):
        wait(f"Fp{j}")
        to_both(f"Fm{j}", f_place(j, z, other))

    def f_block(j, zz):
        row = lax.div(zz, 2) * 2 * rows
        return f_all.at[j, pl.ds(mult(row, rows), 2 * rows), pl.ds(mult(lax.rem(zz, 2) * u, u), u)]

    def do_ff(j):
        wait(f"Fo{j}m", f"Fm{j}m")
        if j in BOTH_WAYS:
            got[f"Ff{j}+"] = push(f_place(j, mate, 0), f_place(j, mate, 0), z_outer)
            wait(f"Fo{j}o", f"Fm{j}o")
            got[f"Ff{j}-"] = push(f_place(j, outer, 1), f_place(j, outer, 1), z_mate)
        else:
            got[f"Ff{j}+"] = push(f_block(j, mate), f_block(j, mate), z_outer)

    def do_fd(j):
        wait(f"Ff{j}+", f"Ff{j}-" if j in BOTH_WAYS else f"Ff{j}+", f"Fo{j}o", f"Fm{j}o")
        f_high[j], f_low[j] = split(f_all[j])

    across, right, left = lax.rem(y + 2, 4), lax.rem(y + 1, 4), lax.rem(y + 3, 4)

    def sum_far(name, j, part, far, half):
        upper, lower = pl.ds(0, half), pl.ds(half, half)
        got[f"{name}{j}f+"] = push(part.at[j, across, upper], far.at[j, 0], y_right)
        got[f"{name}{j}f-"] = push(part.at[j, across, lower], far.at[j, 1], y_left)

    def sum_near(name, j, part, near, half):
        upper, lower = pl.ds(0, half), pl.ds(half, half)
        got[f"{name}{j}n+"] = push(part.at[j, right, lower], near.at[j, 0, lower], y_right)
        got[f"{name}{j}n-"] = push(part.at[j, left, upper], near.at[j, 1, upper], y_left)

    def sum_add(name, j, part, far, near, half):
        upper, lower = pl.ds(0, half), pl.ds(half, half)
        wait(f"{name}{j}f+")
        part[j, right, upper] = part[j, right, upper] + far[j, 0]
        got[f"{name}{j}a+"] = push(part.at[j, right, upper], near.at[j, 0, upper], y_right)
        wait(f"{name}{j}f-")
        part[j, left, lower] = part[j, left, lower] + far[j, 1]
        got[f"{name}{j}a-"] = push(part.at[j, left, lower], near.at[j, 1, lower], y_left)

    def total(name, j, part, near):
        wait(f"{name}{j}n+", f"{name}{j}n-", f"{name}{j}a+", f"{name}{j}a-")
        return part[j, y] + near[j, 0] + near[j, 1]

    def product1(c, blocks):
        j, part = c // 2, pl.ds((c % 2) * u, u)
        for block in blocks:
            p1[c, block] = dot3(a_high[block, part], a_low[block, part], f_high[j], f_low[j])

    def do_m1(c):
        product1(c, (across,))
        sum_far("R1", c, p1, far1, w)

    def do_m1r(c):
        product1(c, (right, left, y))
        sum_near("R1", c, p1, near1, w)

    def do_r1a(c):
        sum_add("R1", c, p1, far1, near1, w)

    z_first = fresh(2 * CHUNKS)
    z_send = fresh(2 * CHUNKS)
    g_first = fresh(4 * CHUNKS)
    g_send = fresh(4 * CHUNKS)

    def place_out(src, dst, lane, send, recv):
        move(jnp.logical_and(k == l, l == lane), src, dst, at(x, y, 2 * h + lane, l), send, recv)

    def do_t1(c):
        j, a = c // 2, c % 2
        value = -total("R1", c, p1, near1)
        z_own[j, pl.ds(a * u, u)] = value
        turned = jnp.transpose(value)
        for piece in range(4):
            z_turn[c, piece] = turned[piece * w : (piece + 1) * w]
        spot = z_all.at[j, x, :, pl.ds(mult(z * rows + a * u, u), u)]
        spot[...] = z_turn[c, z]
        for name, d in (("2", lax.rem(z + 2, 4)), ("m", mate), ("o", outer)):
            got[f"Zs{c}{name}"] = push(z_turn.at[c, d], spot, at(x, y, d, k))
        mine = f_all[j, pl.ds(mult(z * rows + a * u, u), u)]
        c_part[pl.ds(j, 1)] = c_part[pl.ds(j, 1)] - jnp.sum(value * mine, axis=0, keepdims=True)

    def do_zo(j):
        for lane in range(2):
            place_out(
                z_own.at[j, :, pl.ds(lane * u, u)],
                z_stage.at[k, j],
                lane,
                z_send + j * 2 + lane,
                z_first + k * CHUNKS + j,
            )

    def z_half(c, xx, half):
        return z_all.at[c // 2, lax.rem(xx, 4), pl.ds((c % 2) * (w // 2), w // 2), pl.ds(half * 4 * u, 4 * u)]

    def do_zn(c):
        wait(*(f"Zs{c // 2 * 2 + a}{name}" for a in range(2) for name in "2mo"))
        for half in range(2):
            ring_half(f"Zn{c}{half}", z_half(c, x, half), x_right, x_left)

    def do_zf(c):
        wait(f"Zn{c}0+")
        got[f"Zf{c}+"] = push(z_half(c, x + 3, 0), z_half(c, x + 3, 0), x_right)
        wait(f"Zn{c}1-")
        got[f"Zf{c}-"] = push(z_half(c, x + 1, 1), z_half(c, x + 1, 1), x_left)

    def do_zd(c):
        wait(f"Zn{c}1+", f"Zn{c}0-", f"Zf{c}+", f"Zf{c}-")
        v = w // 2
        for xx in range(4):
            part = z_all[c // 2, xx, pl.ds((c % 2) * v, v)]
            zh[c, pl.ds(xx * v, v)], zl[c, pl.ds(xx * v, v)] = split(part)

    def do_m2(c):
        v = w // 2
        for q in range(CHUNKS):
            value = dot3(zh[c], zl[c], f_high[q], f_low[q])
            for block in range(4):
                for lane in range(2):
                    p2[c, block, :, pl.ds((lane * CHUNKS + q) * u, u)] = value[
                        block * v : (block + 1) * v, lane * u : (lane + 1) * u
                    ]
        sum_far("R2", c, p2, far2, v // 2)
        sum_near("R2", c, p2, near2, v // 2)

    def do_r2a(c):
        sum_add("R2", c, p2, far2, near2, w // 4)

    def do_t2(c):
        g_own[c] = total("R2", c, p2, near2)
        for lane in range(2):
            place_out(
                g_own.at[c, :, pl.ds(lane * 4 * u, 4 * u)],
                g_stage.at[k, pl.ds(c * (w // 2), w // 2)],
                lane,
                g_send + c * 2 + lane,
                g_first + k * 2 * CHUNKS + c,
            )

    def prepare_diagonals():
        eye = lax.broadcasted_iota(jnp.int32, (rows, rows), 0) == lax.broadcasted_iota(jnp.int32, (rows, rows), 1)

        def diagonal(tile):
            return jnp.sum(jnp.where(eye, tile, 0.0), axis=0, keepdims=True)

        dd_send[...] = jnp.zeros_like(dd_send)
        dd_send[0, pl.ds(0, 1)] = diagonal(anc_ref[:, own_lanes])
        dd_send[1, pl.ds(0, 1)] = diagonal(diag_ref[other, :, own_lanes])
        dd_send[2, pl.ds(0, 1)] = diagonal(diag_ref[k, :, own_lanes])
        got["Da"] = push(dd_send.at[0], dd_recv.at[0], z_mate)
        got["Dd"] = push(dd_send.at[1], dd_recv.at[1], sibling)

    def start_sums():
        wait("Da", "Dd")
        zd[...] = jnp.where(l == h, dd_send[0], dd_recv[0])
        scale = jnp.logical_and(x == y, l == h).astype(f32)
        mine = dd_send[2, pl.ds(0, 1)]
        theirs = dd_recv[1, pl.ds(0, 1)]
        first = jnp.where(k == 0, mine, theirs) * scale
        last = jnp.where(k == 0, theirs, mine) * scale
        c_part[...] = jnp.zeros_like(c_part)
        for pair in range(2):
            woven = weave(first[:, pair * u : (pair + 1) * u], last[:, pair * u : (pair + 1) * u])
            for i in range(2):
                for lane in range(2):
                    c_part[pl.ds(2 * pair + i, 1), pl.ds(lane * u, u)] = woven[i] * (l == lane).astype(f32)

    def do_ca():
        for d in (1, 2, 3):
            got[f"Ca{d}"] = push(c_part, c_plane.at[d - 1], at(x, y, z + d, k))

    def do_cb():
        wait("Ca1", "Ca2", "Ca3")
        c_line[0] = c_part[...] + c_plane[0] + (c_plane[1] + c_plane[2])
        for d in (1, 2, 3):
            got[f"Cb{d}"] = push(c_line.at[0], c_line.at[d], at(x, y + d, z, k))

    def do_cc():
        wait("Cb1", "Cb2", "Cb3")
        c_front[...] = c_line[0] + c_line[1] + (c_line[2] + c_line[3])
        c_all[x, k] = c_front[...]
        got["Cc"] = push(c_front, c_all.at[x, k], sibling)

    def do_cd():
        wait("Cc")
        c_all[x, 2] = zd[...]
        for d in (1, 2, 3):
            got[f"Cd{d}"] = push(c_all.at[x], c_all.at[x], at(x + d, y, z, k))

    def columns(xx, front, lane):
        blocks = [c_all[xx, front, pl.ds(q, 1), pl.ds(mult(lane * u, u), u)] for q in range(CHUNKS)]
        woven = [weave(blocks[2 * pair], blocks[2 * pair + 1]) for pair in range(2)]
        return jnp.concatenate([woven[0][0], woven[1][0]], axis=1), jnp.concatenate([woven[0][1], woven[1][1]], axis=1)

    def prepare_edges():
        one_hot(u, near_ref, far_ref, hot_near, hot_far)
        bits = u.bit_length() - 1
        step = lax.broadcasted_iota(jnp.int32, (4 * u, near_ref.shape[1]), 0)
        column = ((step >> (bits - 1)) & 1) * 2 * u + (step >> bits) * w + (step & (w - 1))
        for front in range(2):
            near = near_ref[pl.ds(front, 1), :] - lax.axis_index("col") * 4 * u
            hot_stage[front] = (column == near).astype(f32).astype(jnp.bfloat16)

    def do_ce():
        wait("Cd1", "Cd2", "Cd3")
        for front in range(2):
            table[...] = jnp.zeros_like(table)
            first, last = columns(x, front, l)
            table[pl.ds(0, 1), pl.ds(0, rows)] = first
            table[pl.ds(0, 1), pl.ds(rows, rows)] = last
            near = pick(table[...], hot_near[front])
            first, last = columns(y, front, h)
            table[pl.ds(0, 1), pl.ds(0, rows)] = jnp.where(k == 0, first, last)
            table[pl.ds(0, 1), pl.ds(rows, rows)] = c_all[y, 2, pl.ds(0, 1)]
            far = pick(table[...], hot_far[front].astype(jnp.bfloat16))
            r_part[pl.ds(front, 1)] = near[0:1] + far[0:1]

    def finish_z():
        for front in range(2):
            for j in range(CHUNKS):
                arrived(z_stage.at[front, j], z_first + front * CHUNKS + j)
            for pair in range(2):
                woven = weave(z_stage[front, 2 * pair], z_stage[front, 2 * pair + 1])
                for i in range(2):
                    z_out[front, :, pl.ds((2 * i + pair) * u, u)] = woven[i]
            chosen = pick(z_out[front], hot_near[front]) * hot_far[front, pl.ds(rows, rows)]
            chosen = chosen + pick(diag_ref[front], hot_near[front]) * hot_far[front, pl.ds(0, rows)]
            r_part[pl.ds(front, 1)] = r_part[pl.ds(front, 1)] - 2.0 * jnp.sum(chosen, axis=0, keepdims=True)

    def finish_g():
        for front in range(2):
            for c in range(2 * CHUNKS):
                arrived(g_stage.at[front, pl.ds(c * (w // 2), w // 2)], g_first + front * 2 * CHUNKS + c)
            chosen = pick(g_stage[front], hot_stage[front]) * hot_far[front, pl.ds(0, rows)]
            r_out[pl.ds(front, 1)] = r_part[pl.ds(front, 1)] + 2.0 * jnp.sum(chosen, axis=0, keepdims=True)
            for pair in range(2):
                woven = weave(
                    g_stage[front, :, pl.ds(2 * pair * u, u)], g_stage[front, :, pl.ds((2 * pair + 1) * u, u)]
                )
                for i in range(2):
                    lanes = pl.ds((2 * i + pair) * u, u)
                    g_out[front, :, lanes] = diag_ref[front, :, lanes] - woven[i]

    steps = {
        "Ap": do_ap, "Ao": do_ao, "Am": do_am, "Ar": do_ar, "Al": do_al, "Aq": do_aq, "At": do_at, "Ad": do_ad,
        "Fp": do_fp, "Fo": do_fo, "Fm": do_fm, "Ff": do_ff, "Fd": do_fd,
        "M1": do_m1, "M1r": do_m1r, "R1a": do_r1a, "T1": do_t1,
        "Zo": do_zo, "Zn": do_zn, "Zf": do_zf, "Zd": do_zd,
        "M2": do_m2, "R2a": do_r2a, "T2": do_t2, "Da": prepare_diagonals,
        "Ds": start_sums, "Ed": prepare_edges, "Ca": do_ca, "Cb": do_cb, "Cc": do_cc, "Cd": do_cd, "Ce": do_ce,
        "Ez": finish_z,
    }
    turn_ancestor()
    mask_factor()
    pl.semaphore_wait(barrier, len(greet))
    for step in ORDER:
        if step in steps:
            steps[step]()
        else:
            steps[step[:-1]](int(step[-1]))
    finish_g()

    for here, copy in moves:

        @pl.when(jnp.logical_not(here))
        def _():
            copy.wait_send()

    for copy in sent:
        copy.wait_send()


def per_device(anc_inverse, off_factor, diag_inverse, block_mask, edge_child, edge_other):
    fronts, rows, width = off_factor.shape
    edges = edge_child.shape[1]
    u = rows // 2
    w = u // 2
    n = CHUNKS
    f32, bf16 = jnp.float32, jnp.bfloat16
    vmem = pl.BlockSpec(memory_space=pltpu.VMEM)
    m, v = 2 * n, w // 2
    scratch = [
        ((n, rows, u), f32),
        ((n, 8 * u, 2 * u), f32),
        ((n, 8 * u, 2 * u), bf16),
        ((n, 8 * u, 2 * u), bf16),
        ((2, rows, rows), f32),
        ((4, rows, 8 * u), f32),
        ((4, rows, 8 * u), bf16),
        ((4, rows, 8 * u), bf16),
        ((m, 4, u, 2 * u), f32),
        ((m, 2, w, 2 * u), f32),
        ((m, 2, u, 2 * u), f32),
        ((n, rows, 2 * u), f32),
        ((m, 4, w, u), f32),
        ((n, 4, w, 8 * u), f32),
        ((m, 4 * v, 8 * u), bf16),
        ((m, 4 * v, 8 * u), bf16),
        ((2, n, rows, u), f32),
        ((m, 4, v, 8 * u), f32),
        ((m, 2, v // 2, 8 * u), f32),
        ((m, 2, v, 8 * u), f32),
        ((m, v, 8 * u), f32),
        ((2, rows, 4 * u), f32),
        ((3, 8, rows), f32),
        ((2, 8, rows), f32),
        ((8, rows), f32),
        ((3, 8, rows), f32),
        ((4, 8, rows), f32),
        ((8, rows), f32),
        ((4, 3, 8, rows), f32),
        ((8, rows), f32),
        ((8, 4 * u), f32),
        ((2, 4 * u, edges), bf16),
        ((2, 4 * u, edges), f32),
        ((2, 4 * u, edges), bf16),
        ((8, edges), f32),
    ]
    flops = 2 * 3 * 2 * (8 * u) ** 3
    wide = pltpu.VMEM((fronts, rows, width), f32)
    return pl.pallas_call(
        functools.partial(kernel, u),
        out_shape=(wide, wide, pltpu.VMEM((fronts, edges), f32)),
        in_specs=[pl.BlockSpec(memory_space=pltpu.SMEM)] + [vmem] * 5,
        out_specs=(vmem, vmem, vmem),
        scratch_shapes=[pltpu.VMEM(*entry) for entry in scratch]
        + [pltpu.SemaphoreType.DMA((SEMAPHORES,)), pltpu.SemaphoreType.DMA((SEMAPHORES,))],
        compiler_params=pltpu.CompilerParams(collective_id=0, has_side_effects=True, vmem_limit_bytes=54 << 20),
        cost_estimate=pl.CostEstimate(flops=flops, bytes_accessed=5 << 20, transcendentals=0),
    )(block_mask, anc_inverse, off_factor, diag_inverse, edge_child, edge_other)


def solution(mesh):
    placed = (
        P("row", "col"),
        P(None, "row", "col"),
        P(None, "row", "col"),
        P(None, "row"),
        P(None, ("row", "col")),
        P(None, ("row", "col")),
    )
    return jax.shard_map(
        per_device,
        mesh=mesh,
        in_specs=placed,
        out_specs=(P(None, "row", "col"), P(None, "row", "col"), P(None, ("row", "col"))),
        check_vma=False,
    )
```

```python
import functools

import jax
import jax.numpy as jnp
from jax import lax
from jax.experimental import pallas as pl
from jax.experimental.pallas import tpu as pltpu
from jax.sharding import PartitionSpec as P

MESH = pl.DeviceIdType.MESH
CHUNKS = 4
SEMAPHORES = 384
BOTH_WAYS = (0, 1, 2, 3)

ORDER = (
    "Ap1", "Ao1", "Ap0", "Am1", "Fp2", "Fo1", "Fp1", "Ar1", "Fm1", "Ao0", "Ed", "Al1", "Am0", "Fo2", "Aq1", "Ff1", "Da", "Ar0", "At1", "Al0",
    "Fp0", "Fm2", "Aq0", "Ad1", "Fd1", "M13", "Fo0", "M1r3", "At0", "Ff2", "R1a3", "Ad0", "M12", "Fp3", "Ds", "M1r2", "Fm0", "R1a2", "Fo3",
    "Fd2", "M14", "M15", "M1r4", "Ff0", "M1r5", "R1a5", "Fm3", "R1a4", "Fd0", "M10", "T12", "M11", "T13", "M1r1", "Ff3", "M1r0", "R1a0",
    "R1a1", "Zn3", "T15", "T14", "Fd3", "Zn2", "M16", "M17", "M1r7", "Zf3", "M1r6", "T11", "Zn5", "R1a6", "Zo2", "T10", "R1a7", "Zd3", "Zf2",
    "M23", "Zn4", "Zd2", "M22", "Zf5", "Zf4", "T16", "R2a3", "Zn0", "Zd5", "M25", "Zd4", "Zn1", "R2a2", "T17", "Ca", "Zo1", "Zf0", "M24",
    "R2a5", "Zf1", "Zn6", "T22", "Zd0", "Zo0", "M20", "R2a4", "Cb", "Zn7", "Zd1", "M21", "Zf6", "Zf7", "R2a0", "Zd6", "Zo3", "M26", "Zd7",
    "T25", "Cc", "T24", "R2a1", "Cd", "T20", "M27", "T23", "Ce", "T21", "R2a6", "R2a7", "T26", "T27", "Ez", "Eg",
)


def place():
    row = lax.axis_index("row")
    col = lax.axis_index("col")
    return lax.div(col, 2), lax.div(row, 4), lax.rem(lax.div(row, 2), 2), lax.rem(col, 2), lax.rem(row, 2)


def at(x, y, z, k):
    x, y, z, k = lax.rem(x, 4), lax.rem(y, 4), lax.rem(z, 4), lax.rem(k, 2)
    return (y * 4 + lax.div(z, 2) * 2 + k, x * 2 + lax.rem(z, 2))


def split(value):
    high = value.astype(jnp.bfloat16)
    return high, (value - high.astype(jnp.float32)).astype(jnp.bfloat16)


def dot3(left_high, left_low, right_high, right_low):
    def dot(left, right):
        return jnp.dot(left, right, preferred_element_type=jnp.float32)

    return dot(left_high, right_high) + (dot(left_high, right_low) + dot(left_low, right_high))


def pick(value, hot):
    high, rest = split(value)
    low = value - high.astype(jnp.float32) - rest.astype(jnp.float32)
    parts = (high, rest, low.astype(jnp.bfloat16))
    return sum(jnp.dot(part, hot, preferred_element_type=jnp.float32) for part in parts)


def weave(first, second):
    half = first.shape[1] // 2
    low = lax.broadcasted_iota(jnp.int32, first.shape, 1) < half
    return (
        jnp.where(low, first, pltpu.roll(second, half, 1)),
        jnp.where(low, pltpu.roll(first, half, 1), second),
    )


def one_hot(u, near_ref, far_ref, hot_near, hot_far):
    rows = 2 * u
    for front in range(2):
        step = lax.broadcasted_iota(jnp.int32, (4 * u, near_ref.shape[1]), 0)
        near = near_ref[pl.ds(front, 1), :] - lax.axis_index("col") * 4 * u
        far = far_ref[pl.ds(front, 1), :]
        start = lax.axis_index("row") * rows
        far = jnp.where(far < 32 * u, far - start, far - 32 * u - start + rows)
        hot_near[front] = (step == near).astype(jnp.float32).astype(jnp.bfloat16)
        hot_far[front] = (step == far).astype(jnp.float32)


def kernel(
    u,
    mask_ref,
    anc_given,
    fac_given,
    diag_given,
    near_ref,
    far_ref,
    z_out,
    g_out,
    r_out,
    f_send,
    f_all,
    f_high,
    f_low,
    a_turn,
    a_all,
    a_high,
    a_low,
    p1,
    far1,
    near1,
    z_own,
    z_turn,
    z_all,
    zh,
    zl,
    z_stage,
    p2,
    far2,
    near2,
    g_own,
    g_stage,
    dd_send,
    dd_recv,
    c_part,
    c_plane,
    c_line,
    c_front,
    c_all,
    zd,
    table,
    hot_near,
    hot_far,
    hot_stage,
    r_part,
    anc_ref,
    fac_ref,
    diag_ref,
    load_sems,
    send_sems,
    recv_sems,
):
    x, y, h, l, k = place()
    z = 2 * h + l
    rows = 2 * u
    w = u // 2
    f32 = jnp.float32
    other = 1 - k

    count = [0]

    def fresh(n=1):
        first = count[0]
        count[0] += n
        return first

    def mult(value, of):
        return pl.multiple_of(value, of)

    def remote(src, dst, device, send, recv):
        return pltpu.make_async_remote_copy(
            src_ref=src,
            dst_ref=dst,
            send_sem=send_sems.at[send],
            recv_sem=recv_sems.at[recv],
            device_id=device,
            device_id_type=MESH,
        )

    sent = []

    def push(src, dst, device):
        i = fresh()
        copy = remote(src, dst, device, i, i)
        copy.start()
        sent.append(copy)
        return copy

    sibling = at(x, y, z, k + 1)
    x_right, x_left = at(x + 1, y, z, k), at(x + 3, y, z, k)
    y_right, y_left = at(x, y + 1, z, k), at(x, y + 3, z, k)
    mate, outer = 2 * h + 1 - l, lax.rem(z + 3 + 2 * l, 4)
    z_mate, z_outer, z_across = at(x, y, mate, k), at(x, y, outer, k), at(x, y, z + 2, k)

    barrier = pltpu.get_barrier_semaphore()
    greet = (z_across, z_outer, z_mate, sibling, x_right, x_left, y_right, y_left)
    for device in greet:
        pl.semaphore_signal(barrier, inc=1, device_id=device, device_id_type=MESH)
    pairs = ((anc_given, anc_ref), (fac_given, fac_ref), (diag_given, diag_ref))
    loads = [pltpu.make_async_copy(given, here, load_sems.at[i]) for i, (given, here) in enumerate(pairs)]
    for load in loads:
        load.start()

    own_lanes = pl.ds(mult(k * rows, rows), rows)

    def a_place(xx, hh, kk, a):
        lanes = pl.ds(mult((hh * 2 + kk) * rows, rows), rows)
        return a_all.at[lax.rem(xx, 4), pl.ds(a * u, u), lanes]

    def turn_ancestor():
        for half in range(2):
            a_turn[half] = jnp.transpose(anc_ref[:, half * rows : (half + 1) * rows])

    def f_place(j, zz, half):
        row = (lax.div(zz, 2) * 2 + half) * rows
        return f_all.at[j, pl.ds(mult(row, rows), rows), pl.ds(mult(lax.rem(zz, 2) * u, u), u)]

    def mask_factor():
        for front, mine in ((other, False), (k, True)):
            for b in range(2):
                source = pl.ds(b * u, u)
                keep = mask_ref[front, b].astype(f32)
                for pair in range(2):
                    woven = weave(
                        fac_ref[front, source, pl.ds(pair * u, u)] * keep,
                        fac_ref[front, source, pl.ds((2 + pair) * u, u)] * keep,
                    )
                    for i in range(2):
                        if mine:
                            f_place(2 * pair + i, z, k).at[source][...] = woven[i]
                        else:
                            f_send[2 * pair + i, source] = woven[i]

    got = {}
    waited = set()

    def ring_half(name, src, right, left):
        got[name + "+"] = push(src, src, right)
        got[name + "-"] = push(src, src, left)

    def wait(*names):
        for name in names:
            if name not in waited:
                waited.add(name)
                got[name].wait_recv()

    a_first = fresh(4)
    a_sends = fresh(4)
    moves = []

    def move(here, src, dst, device, send, recv):
        copy = remote(src, dst, device, send, recv)
        local = pltpu.make_async_copy(src, dst, recv_sems.at[recv])

        @pl.when(here)
        def _():
            local.start()

        @pl.when(jnp.logical_not(here))
        def _():
            copy.start()

        moves.append((here, copy))

    def arrived(here, sem):
        pltpu.make_async_copy(here, here, recv_sems.at[sem]).wait()

    def to_sibling(a, i, xx, hh):
        got[f"As{a}{i}"] = push(a_place(xx, hh, k, a), a_place(xx, hh, k, a), sibling)

    def do_ap(a):
        for half in range(2):
            here = jnp.logical_and(l == h, l == half)
            move(
                here,
                a_turn.at[half, pl.ds(a * u, u)],
                a_place(x, h, k, a),
                at(x, y, 2 * l + half, k),
                a_sends + a * 2 + half,
                a_first + a * 2 + h,
            )

    def do_ao(a):
        arrived(a_place(x, h, k, a), a_first + a * 2 + h)
        ring_half(f"Ao{a}", a_place(x, h, k, a), x_right, x_left)
        to_sibling(a, 0, x, h)

    def do_am(a):
        arrived(a_place(x, 1 - h, k, a), a_first + a * 2 + 1 - h)
        ring_half(f"Am{a}", a_place(x, 1 - h, k, a), x_right, x_left)
        to_sibling(a, 1, x, 1 - h)

    def do_ar(a):
        wait(f"Ao{a}+")
        got[f"Af{a}+"] = push(a_place(x + 3, h, k, a), a_place(x + 3, h, k, a), x_right)
        to_sibling(a, 2, x + 3, h)

    def do_al(a):
        wait(f"Am{a}-")
        got[f"Af{a}-"] = push(a_place(x + 1, 1 - h, k, a), a_place(x + 1, 1 - h, k, a), x_left)
        to_sibling(a, 3, x + 1, 1 - h)

    def do_aq(a):
        wait(f"Ao{a}-", f"Am{a}+")
        to_sibling(a, 4, x + 1, h)
        to_sibling(a, 5, x + 3, 1 - h)

    def do_at(a):
        wait(f"Af{a}+", f"Af{a}-")
        for hh in range(2):
            to_sibling(a, 6 + hh, x + 2, hh)

    def do_ad(a):
        for i in range(8):
            wait(f"As{a}{i}")
        part = pl.ds(a * u, u)
        for xx in range(4):
            a_high[xx, part], a_low[xx, part] = split(a_all[xx, part])

    def do_fp(j):
        got[f"Fp{j}"] = push(f_send.at[j], f_place(j, z, k), sibling)

    def to_both(name, src):
        got[name + "m"] = push(src, src, z_mate)
        got[name + "o"] = push(src, src, z_outer)

    def do_fo(j):
        to_both(f"Fo{j}", f_place(j, z, k))

    def do_fm(j):
        wait(f"Fp{j}")
        to_both(f"Fm{j}", f_place(j, z, other))

    def f_block(j, zz):
        row = lax.div(zz, 2) * 2 * rows
        return f_all.at[j, pl.ds(mult(row, rows), 2 * rows), pl.ds(mult(lax.rem(zz, 2) * u, u), u)]

    def do_ff(j):
        wait(f"Fo{j}m", f"Fm{j}m")
        if j in BOTH_WAYS:
            got[f"Ff{j}+"] = push(f_place(j, mate, 0), f_place(j, mate, 0), z_outer)
            wait(f"Fo{j}o", f"Fm{j}o")
            got[f"Ff{j}-"] = push(f_place(j, outer, 1), f_place(j, outer, 1), z_mate)
        else:
            got[f"Ff{j}+"] = push(f_block(j, mate), f_block(j, mate), z_outer)

    def do_fd(j):
        wait(f"Ff{j}+", f"Ff{j}-" if j in BOTH_WAYS else f"Ff{j}+", f"Fo{j}o", f"Fm{j}o")
        f_high[j], f_low[j] = split(f_all[j])

    across, right, left = lax.rem(y + 2, 4), lax.rem(y + 1, 4), lax.rem(y + 3, 4)

    def sum_far(name, j, part, far, half):
        upper, lower = pl.ds(0, half), pl.ds(half, half)
        got[f"{name}{j}f+"] = push(part.at[j, across, upper], far.at[j, 0], y_right)
        got[f"{name}{j}f-"] = push(part.at[j, across, lower], far.at[j, 1], y_left)

    def sum_near(name, j, part, near, half):
        upper, lower = pl.ds(0, half), pl.ds(half, half)
        got[f"{name}{j}n+"] = push(part.at[j, right, lower], near.at[j, 0, lower], y_right)
        got[f"{name}{j}n-"] = push(part.at[j, left, upper], near.at[j, 1, upper], y_left)

    def sum_add(name, j, part, far, near, half):
        upper, lower = pl.ds(0, half), pl.ds(half, half)
        wait(f"{name}{j}f+")
        part[j, right, upper] = part[j, right, upper] + far[j, 0]
        got[f"{name}{j}a+"] = push(part.at[j, right, upper], near.at[j, 0, upper], y_right)
        wait(f"{name}{j}f-")
        part[j, left, lower] = part[j, left, lower] + far[j, 1]
        got[f"{name}{j}a-"] = push(part.at[j, left, lower], near.at[j, 1, lower], y_left)

    def total(name, j, part, near):
        wait(f"{name}{j}n+", f"{name}{j}n-", f"{name}{j}a+", f"{name}{j}a-")
        return part[j, y] + near[j, 0] + near[j, 1]

    def product1(c, blocks):
        j, part = c // 2, pl.ds((c % 2) * u, u)
        for block in blocks:
            p1[c, block] = dot3(a_high[block, part], a_low[block, part], f_high[j], f_low[j])

    def do_m1(c):
        product1(c, (across,))
        sum_far("R1", c, p1, far1, w)

    def do_m1r(c):
        product1(c, (right, left, y))
        sum_near("R1", c, p1, near1, w)

    def do_r1a(c):
        sum_add("R1", c, p1, far1, near1, w)

    z_first = fresh(2 * CHUNKS)
    z_send = fresh(2 * CHUNKS)
    g_first = fresh(4 * CHUNKS)
    g_send = fresh(4 * CHUNKS)

    def place_out(src, dst, lane, send, recv):
        move(jnp.logical_and(k == l, l == lane), src, dst, at(x, y, 2 * h + lane, l), send, recv)

    def do_t1(c):
        j, a = c // 2, c % 2
        value = -total("R1", c, p1, near1)
        z_own[j, pl.ds(a * u, u)] = value
        turned = jnp.transpose(value)
        for piece in range(4):
            z_turn[c, piece] = turned[piece * w : (piece + 1) * w]
        spot = z_all.at[j, x, :, pl.ds(mult(z * rows + a * u, u), u)]
        spot[...] = z_turn[c, z]
        for name, d in (("2", lax.rem(z + 2, 4)), ("m", mate), ("o", outer)):
            got[f"Zs{c}{name}"] = push(z_turn.at[c, d], spot, at(x, y, d, k))
        mine = f_all[j, pl.ds(mult(z * rows + a * u, u), u)]
        c_part[pl.ds(j, 1)] = c_part[pl.ds(j, 1)] - jnp.sum(value * mine, axis=0, keepdims=True)

    def do_zo(j):
        for lane in range(2):
            place_out(
                z_own.at[j, :, pl.ds(lane * u, u)],
                z_stage.at[k, j],
                lane,
                z_send + j * 2 + lane,
                z_first + k * CHUNKS + j,
            )

    def z_half(c, xx, half):
        return z_all.at[c // 2, lax.rem(xx, 4), pl.ds((c % 2) * (w // 2), w // 2), pl.ds(half * 4 * u, 4 * u)]

    def do_zn(c):
        wait(*(f"Zs{c // 2 * 2 + a}{name}" for a in range(2) for name in "2mo"))
        for half in range(2):
            ring_half(f"Zn{c}{half}", z_half(c, x, half), x_right, x_left)

    def do_zf(c):
        wait(f"Zn{c}0+")
        got[f"Zf{c}+"] = push(z_half(c, x + 3, 0), z_half(c, x + 3, 0), x_right)
        wait(f"Zn{c}1-")
        got[f"Zf{c}-"] = push(z_half(c, x + 1, 1), z_half(c, x + 1, 1), x_left)

    def do_zd(c):
        wait(f"Zn{c}1+", f"Zn{c}0-", f"Zf{c}+", f"Zf{c}-")
        v = w // 2
        for xx in range(4):
            part = z_all[c // 2, xx, pl.ds((c % 2) * v, v)]
            zh[c, pl.ds(xx * v, v)], zl[c, pl.ds(xx * v, v)] = split(part)

    def do_m2(c):
        v = w // 2
        for q in range(CHUNKS):
            value = dot3(zh[c], zl[c], f_high[q], f_low[q])
            for block in range(4):
                for lane in range(2):
                    p2[c, block, :, pl.ds((lane * CHUNKS + q) * u, u)] = value[
                        block * v : (block + 1) * v, lane * u : (lane + 1) * u
                    ]
        sum_far("R2", c, p2, far2, v // 2)
        sum_near("R2", c, p2, near2, v // 2)

    def do_r2a(c):
        sum_add("R2", c, p2, far2, near2, w // 4)

    def do_t2(c):
        g_own[c] = total("R2", c, p2, near2)
        for lane in range(2):
            place_out(
                g_own.at[c, :, pl.ds(lane * 4 * u, 4 * u)],
                g_stage.at[k, pl.ds(c * (w // 2), w // 2)],
                lane,
                g_send + c * 2 + lane,
                g_first + k * 2 * CHUNKS + c,
            )

    def prepare_diagonals():
        eye = lax.broadcasted_iota(jnp.int32, (rows, rows), 0) == lax.broadcasted_iota(jnp.int32, (rows, rows), 1)

        def diagonal(tile):
            return jnp.sum(jnp.where(eye, tile, 0.0), axis=0, keepdims=True)

        dd_send[...] = jnp.zeros_like(dd_send)
        dd_send[0, pl.ds(0, 1)] = diagonal(anc_ref[:, own_lanes])
        dd_send[1, pl.ds(0, 1)] = diagonal(diag_ref[other, :, own_lanes])
        dd_send[2, pl.ds(0, 1)] = diagonal(diag_ref[k, :, own_lanes])
        got["Da"] = push(dd_send.at[0], dd_recv.at[0], z_mate)
        got["Dd"] = push(dd_send.at[1], dd_recv.at[1], sibling)

    def start_sums():
        wait("Da", "Dd")
        zd[...] = jnp.where(l == h, dd_send[0], dd_recv[0])
        scale = jnp.logical_and(x == y, l == h).astype(f32)
        mine = dd_send[2, pl.ds(0, 1)]
        theirs = dd_recv[1, pl.ds(0, 1)]
        first = jnp.where(k == 0, mine, theirs) * scale
        last = jnp.where(k == 0, theirs, mine) * scale
        c_part[...] = jnp.zeros_like(c_part)
        for pair in range(2):
            woven = weave(first[:, pair * u : (pair + 1) * u], last[:, pair * u : (pair + 1) * u])
            for i in range(2):
                for lane in range(2):
                    c_part[pl.ds(2 * pair + i, 1), pl.ds(lane * u, u)] = woven[i] * (l == lane).astype(f32)

    def do_ca():
        for d in (1, 2, 3):
            got[f"Ca{d}"] = push(c_part, c_plane.at[d - 1], at(x, y, z + d, k))

    def do_cb():
        wait("Ca1", "Ca2", "Ca3")
        c_line[0] = c_part[...] + c_plane[0] + (c_plane[1] + c_plane[2])
        for d in (1, 2, 3):
            got[f"Cb{d}"] = push(c_line.at[0], c_line.at[d], at(x, y + d, z, k))

    def do_cc():
        wait("Cb1", "Cb2", "Cb3")
        c_front[...] = c_line[0] + c_line[1] + (c_line[2] + c_line[3])
        c_all[x, k] = c_front[...]
        got["Cc"] = push(c_front, c_all.at[x, k], sibling)

    def do_cd():
        wait("Cc")
        c_all[x, 2] = zd[...]
        for d in (1, 2, 3):
            got[f"Cd{d}"] = push(c_all.at[x], c_all.at[x], at(x + d, y, z, k))

    def columns(xx, front, lane):
        blocks = [c_all[xx, front, pl.ds(q, 1), pl.ds(mult(lane * u, u), u)] for q in range(CHUNKS)]
        woven = [weave(blocks[2 * pair], blocks[2 * pair + 1]) for pair in range(2)]
        return jnp.concatenate([woven[0][0], woven[1][0]], axis=1), jnp.concatenate([woven[0][1], woven[1][1]], axis=1)

    def prepare_edges():
        one_hot(u, near_ref, far_ref, hot_near, hot_far)
        bits = u.bit_length() - 1
        step = lax.broadcasted_iota(jnp.int32, (4 * u, near_ref.shape[1]), 0)
        column = ((step >> (bits - 1)) & 1) * 2 * u + (step >> bits) * w + (step & (w - 1))
        for front in range(2):
            near = near_ref[pl.ds(front, 1), :] - lax.axis_index("col") * 4 * u
            hot_stage[front] = (column == near).astype(f32).astype(jnp.bfloat16)

    def do_ce():
        wait("Cd1", "Cd2", "Cd3")
        for front in range(2):
            table[...] = jnp.zeros_like(table)
            first, last = columns(x, front, l)
            table[pl.ds(0, 1), pl.ds(0, rows)] = first
            table[pl.ds(0, 1), pl.ds(rows, rows)] = last
            near = pick(table[...], hot_near[front])
            first, last = columns(y, front, h)
            table[pl.ds(0, 1), pl.ds(0, rows)] = jnp.where(k == 0, first, last)
            table[pl.ds(0, 1), pl.ds(rows, rows)] = c_all[y, 2, pl.ds(0, 1)]
            far = pick(table[...], hot_far[front].astype(jnp.bfloat16))
            r_part[pl.ds(front, 1)] = near[0:1] + far[0:1]

    def finish_z():
        for front in range(2):
            for j in range(CHUNKS):
                arrived(z_stage.at[front, j], z_first + front * CHUNKS + j)
            for pair in range(2):
                woven = weave(z_stage[front, 2 * pair], z_stage[front, 2 * pair + 1])
                for i in range(2):
                    z_out[front, :, pl.ds((2 * i + pair) * u, u)] = woven[i]
            chosen = pick(z_out[front], hot_near[front]) * hot_far[front, pl.ds(rows, rows)]
            chosen = chosen + pick(diag_ref[front], hot_near[front]) * hot_far[front, pl.ds(0, rows)]
            r_part[pl.ds(front, 1)] = r_part[pl.ds(front, 1)] - 2.0 * jnp.sum(chosen, axis=0, keepdims=True)

    def finish_rows(first, last):
        v = w // 2
        part = pl.ds(first * v, (last - first) * v)
        for front in range(2):
            for c in range(first, last):
                arrived(g_stage.at[front, pl.ds(c * v, v)], g_first + front * 2 * CHUNKS + c)
            chosen = pick(g_stage[front, part], hot_stage[front]) * hot_far[front, part]
            r_part[pl.ds(front, 1)] = r_part[pl.ds(front, 1)] + 2.0 * jnp.sum(chosen, axis=0, keepdims=True)
            for pair in range(2):
                woven = weave(
                    g_stage[front, part, pl.ds(2 * pair * u, u)], g_stage[front, part, pl.ds((2 * pair + 1) * u, u)]
                )
                for i in range(2):
                    lanes = pl.ds((2 * i + pair) * u, u)
                    g_out[front, part, lanes] = diag_ref[front, part, lanes] - woven[i]

    def do_eg():
        finish_rows(0, 2 * CHUNKS - 2)

    steps = {
        "Ap": do_ap, "Ao": do_ao, "Am": do_am, "Ar": do_ar, "Al": do_al, "Aq": do_aq, "At": do_at, "Ad": do_ad,
        "Fp": do_fp, "Fo": do_fo, "Fm": do_fm, "Ff": do_ff, "Fd": do_fd,
        "M1": do_m1, "M1r": do_m1r, "R1a": do_r1a, "T1": do_t1,
        "Zo": do_zo, "Zn": do_zn, "Zf": do_zf, "Zd": do_zd,
        "M2": do_m2, "R2a": do_r2a, "T2": do_t2, "Da": prepare_diagonals,
        "Ds": start_sums, "Ed": prepare_edges, "Ca": do_ca, "Cb": do_cb, "Cc": do_cc, "Cd": do_cd, "Ce": do_ce,
        "Ez": finish_z, "Eg": do_eg,
    }
    loads[0].wait()
    turn_ancestor()
    loads[1].wait()
    mask_factor()
    loads[2].wait()
    pl.semaphore_wait(barrier, len(greet))
    for step in ORDER:
        if step in steps:
            steps[step]()
        else:
            steps[step[:-1]](int(step[-1]))
    finish_rows(2 * CHUNKS - 2, 2 * CHUNKS)
    r_out[...] = r_part[0:2]

    for here, copy in moves:

        @pl.when(jnp.logical_not(here))
        def _():
            copy.wait_send()

    for copy in sent:
        copy.wait_send()


def per_device(anc_inverse, off_factor, diag_inverse, block_mask, edge_child, edge_other):
    fronts, rows, width = off_factor.shape
    edges = edge_child.shape[1]
    u = rows // 2
    w = u // 2
    n = CHUNKS
    f32, bf16 = jnp.float32, jnp.bfloat16
    vmem = pl.BlockSpec(memory_space=pltpu.VMEM)
    m, v = 2 * n, w // 2
    scratch = [
        ((n, rows, u), f32),
        ((n, 8 * u, 2 * u), f32),
        ((n, 8 * u, 2 * u), bf16),
        ((n, 8 * u, 2 * u), bf16),
        ((2, rows, rows), f32),
        ((4, rows, 8 * u), f32),
        ((4, rows, 8 * u), bf16),
        ((4, rows, 8 * u), bf16),
        ((m, 4, u, 2 * u), f32),
        ((m, 2, w, 2 * u), f32),
        ((m, 2, u, 2 * u), f32),
        ((n, rows, 2 * u), f32),
        ((m, 4, w, u), f32),
        ((n, 4, w, 8 * u), f32),
        ((m, 4 * v, 8 * u), bf16),
        ((m, 4 * v, 8 * u), bf16),
        ((2, n, rows, u), f32),
        ((m, 4, v, 8 * u), f32),
        ((m, 2, v // 2, 8 * u), f32),
        ((m, 2, v, 8 * u), f32),
        ((m, v, 8 * u), f32),
        ((2, rows, 4 * u), f32),
        ((3, 8, rows), f32),
        ((2, 8, rows), f32),
        ((8, rows), f32),
        ((3, 8, rows), f32),
        ((4, 8, rows), f32),
        ((8, rows), f32),
        ((4, 3, 8, rows), f32),
        ((8, rows), f32),
        ((8, 4 * u), f32),
        ((2, 4 * u, edges), bf16),
        ((2, 4 * u, edges), f32),
        ((2, 4 * u, edges), bf16),
        ((8, edges), f32),
        (anc_inverse.shape, f32),
        (off_factor.shape, f32),
        (diag_inverse.shape, f32),
    ]
    flops = 2 * 3 * 2 * (8 * u) ** 3
    wide = pltpu.VMEM((fronts, rows, width), f32)
    return pl.pallas_call(
        functools.partial(kernel, u),
        out_shape=(wide, wide, pltpu.VMEM((fronts, edges), f32)),
        in_specs=[pl.BlockSpec(memory_space=pltpu.SMEM)] + [pl.BlockSpec(memory_space=pl.ANY)] * 3 + [vmem] * 2,
        out_specs=(vmem, vmem, vmem),
        scratch_shapes=[pltpu.VMEM(*entry) for entry in scratch]
        + [pltpu.SemaphoreType.DMA((3,)), pltpu.SemaphoreType.DMA((SEMAPHORES,)), pltpu.SemaphoreType.DMA((SEMAPHORES,))],
        compiler_params=pltpu.CompilerParams(collective_id=0, has_side_effects=True, vmem_limit_bytes=54 << 20),
        cost_estimate=pl.CostEstimate(flops=flops, bytes_accessed=5 << 20, transcendentals=0),
    )(block_mask, anc_inverse, off_factor, diag_inverse, edge_child, edge_other)


def solution(mesh):
    placed = (
        P("row", "col"),
        P(None, "row", "col"),
        P(None, "row", "col"),
        P(None, "row"),
        P(None, ("row", "col")),
        P(None, ("row", "col")),
    )
    return jax.shard_map(
        per_device,
        mesh=mesh,
        in_specs=placed,
        out_specs=(P(None, "row", "col"), P(None, "row", "col"), P(None, ("row", "col"))),
        check_vma=False,
    )
```

```python
import functools

import jax
import jax.numpy as jnp
from jax import lax
from jax.experimental import pallas as pl
from jax.experimental.pallas import tpu as pltpu
from jax.sharding import PartitionSpec as P

MESH = pl.DeviceIdType.MESH
CHUNKS = 4
SEMAPHORES = 384
BOTH_WAYS = (0, 1, 2, 3)

ORDER = (
    "Ap1", "Ao1", "Ap0", "Am1", "Fp2", "Fo1", "Fp1", "Ar1", "Fm1", "Ao0", "Ed", "Al1", "Am0", "Fo2", "Aq1", "Ff1", "Da", "Ar0", "At1", "Al0",
    "Fp0", "Fm2", "Aq0", "Ad1", "Fd1", "M13", "Fo0", "M1r3", "At0", "Ff2", "R1a3", "Ad0", "M12", "Fp3", "Ds", "M1r2", "Fm0", "R1a2", "Fo3",
    "Fd2", "M14", "M15", "M1r4", "Ff0", "M1r5", "R1a5", "Fm3", "R1a4", "Fd0", "M10", "T12", "M11", "T13", "M1r1", "Ff3", "M1r0", "R1a0",
    "R1a1", "Zn3", "T15", "T14", "Fd3", "Zn2", "M16", "M17", "M1r7", "Zf3", "M1r6", "T11", "Zn5", "R1a6", "Zo2", "T10", "R1a7", "Zd3", "Zf2",
    "M23", "Zn4", "Zd2", "M22", "Zf5", "Zf4", "T16", "R2a3", "Zn0", "Zd5", "M25", "Zd4", "Zn1", "R2a2", "T17", "Ca", "Zo1", "Zf0", "M24",
    "R2a5", "Zf1", "Zn6", "T22", "Zd0", "Zo0", "M20", "R2a4", "Cb", "Zn7", "Zd1", "M21", "Zf6", "Zf7", "R2a0", "Zd6", "Zo3", "M26", "Zd7",
    "T25", "Cc", "T24", "R2a1", "Cd", "T20", "M27", "T23", "Ce", "T21", "R2a6", "R2a7", "T26", "T27", "Ez", "Eg",
)


def place():
    row = lax.axis_index("row")
    col = lax.axis_index("col")
    return lax.div(col, 2), lax.div(row, 4), lax.rem(lax.div(row, 2), 2), lax.rem(col, 2), lax.rem(row, 2)


def at(x, y, z, k):
    x, y, z, k = lax.rem(x, 4), lax.rem(y, 4), lax.rem(z, 4), lax.rem(k, 2)
    return (y * 4 + lax.div(z, 2) * 2 + k, x * 2 + lax.rem(z, 2))


def split(value):
    high = value.astype(jnp.bfloat16)
    return high, (value - high.astype(jnp.float32)).astype(jnp.bfloat16)


def dot3(left_high, left_low, right_high, right_low):
    def dot(left, right):
        return jnp.dot(left, right, preferred_element_type=jnp.float32)

    return dot(left_high, right_high) + (dot(left_high, right_low) + dot(left_low, right_high))


def pick(value, hot):
    high, rest = split(value)
    low = value - high.astype(jnp.float32) - rest.astype(jnp.float32)
    parts = (high, rest, low.astype(jnp.bfloat16))
    return sum(jnp.dot(part, hot, preferred_element_type=jnp.float32) for part in parts)


def weave(first, second):
    half = first.shape[1] // 2
    low = lax.broadcasted_iota(jnp.int32, first.shape, 1) < half
    return (
        jnp.where(low, first, pltpu.roll(second, half, 1)),
        jnp.where(low, pltpu.roll(first, half, 1), second),
    )


def one_hot(u, near_ref, far_ref, hot_near, hot_far):
    rows = 2 * u
    for front in range(2):
        step = lax.broadcasted_iota(jnp.int32, (4 * u, near_ref.shape[1]), 0)
        near = near_ref[pl.ds(front, 1), :] - lax.axis_index("col") * 4 * u
        far = far_ref[pl.ds(front, 1), :]
        start = lax.axis_index("row") * rows
        far = jnp.where(far < 32 * u, far - start, far - 32 * u - start + rows)
        hot_near[front] = (step == near).astype(jnp.float32).astype(jnp.bfloat16)
        hot_far[front] = (step == far).astype(jnp.float32)


def kernel(
    u,
    mask_ref,
    anc_given,
    fac_given,
    diag_given,
    near_ref,
    far_ref,
    z_out,
    g_out,
    r_out,
    f_send,
    f_all,
    f_high,
    f_low,
    a_turn,
    a_all,
    a_high,
    a_low,
    p1,
    far1,
    near1,
    z_own,
    z_turn,
    z_all,
    zh,
    zl,
    z_stage,
    p2,
    far2,
    near2,
    g_own,
    g_stage,
    dd_send,
    dd_recv,
    c_part,
    c_plane,
    c_line,
    c_front,
    c_all,
    zd,
    table,
    hot_near,
    hot_far,
    hot_stage,
    r_part,
    anc_ref,
    fac_ref,
    diag_ref,
    load_sems,
    send_sems,
    recv_sems,
):
    x, y, h, l, k = place()
    z = 2 * h + l
    rows = 2 * u
    w = u // 2
    f32 = jnp.float32
    other = 1 - k

    count = [0]

    def fresh(n=1):
        first = count[0]
        count[0] += n
        return first

    def mult(value, of):
        return pl.multiple_of(value, of)

    def remote(src, dst, device, send, recv):
        return pltpu.make_async_remote_copy(
            src_ref=src,
            dst_ref=dst,
            send_sem=send_sems.at[send],
            recv_sem=recv_sems.at[recv],
            device_id=device,
            device_id_type=MESH,
        )

    sent = []

    def push(src, dst, device):
        i = fresh()
        copy = remote(src, dst, device, i, i)
        copy.start()
        sent.append(copy)
        return copy

    sibling = at(x, y, z, k + 1)
    x_right, x_left = at(x + 1, y, z, k), at(x + 3, y, z, k)
    y_right, y_left = at(x, y + 1, z, k), at(x, y + 3, z, k)
    mate, outer = 2 * h + 1 - l, lax.rem(z + 3 + 2 * l, 4)
    z_mate, z_outer, z_across = at(x, y, mate, k), at(x, y, outer, k), at(x, y, z + 2, k)

    barrier = pltpu.get_barrier_semaphore()
    greet = (z_across, z_outer, z_mate, sibling, x_right, x_left, y_right, y_left)
    for device in greet:
        pl.semaphore_signal(barrier, inc=1, device_id=device, device_id_type=MESH)
    pairs = ((anc_given, anc_ref), (fac_given, fac_ref), (diag_given, diag_ref))
    loads = [pltpu.make_async_copy(given, here, load_sems.at[i]) for i, (given, here) in enumerate(pairs)]
    for load in loads:
        load.start()

    own_lanes = pl.ds(mult(k * rows, rows), rows)

    def a_place(xx, hh, kk, a):
        lanes = pl.ds(mult((hh * 2 + kk) * rows, rows), rows)
        return a_all.at[lax.rem(xx, 4), pl.ds(a * u, u), lanes]

    def turn_ancestor():
        for half in range(2):
            a_turn[half] = jnp.transpose(anc_ref[:, half * rows : (half + 1) * rows])

    def f_place(j, zz, half):
        row = (lax.div(zz, 2) * 2 + half) * rows
        return f_all.at[j, pl.ds(mult(row, rows), rows), pl.ds(mult(lax.rem(zz, 2) * u, u), u)]

    def mask_factor():
        for front, mine in ((other, False), (k, True)):
            for b in range(2):
                source = pl.ds(b * u, u)
                keep = mask_ref[front, b].astype(f32)
                for pair in range(2):
                    woven = weave(
                        fac_ref[front, source, pl.ds(pair * u, u)] * keep,
                        fac_ref[front, source, pl.ds((2 + pair) * u, u)] * keep,
                    )
                    for i in range(2):
                        if mine:
                            f_place(2 * pair + i, z, k).at[source][...] = woven[i]
                        else:
                            f_send[2 * pair + i, source] = woven[i]

    got = {}
    waited = set()

    def ring_half(name, src, right, left):
        got[name + "+"] = push(src, src, right)
        got[name + "-"] = push(src, src, left)

    def wait(*names):
        for name in names:
            if name not in waited:
                waited.add(name)
                got[name].wait_recv()

    a_first = fresh(4)
    a_sends = fresh(4)
    moves = []

    def move(here, src, dst, device, send, recv):
        copy = remote(src, dst, device, send, recv)
        local = pltpu.make_async_copy(src, dst, recv_sems.at[recv])

        @pl.when(here)
        def _():
            local.start()

        @pl.when(jnp.logical_not(here))
        def _():
            copy.start()

        moves.append((here, copy))

    def arrived(here, sem):
        pltpu.make_async_copy(here, here, recv_sems.at[sem]).wait()

    def to_sibling(a, i, xx, hh):
        got[f"As{a}{i}"] = push(a_place(xx, hh, k, a), a_place(xx, hh, k, a), sibling)

    def do_ap(a):
        for half in range(2):
            here = jnp.logical_and(l == h, l == half)
            move(
                here,
                a_turn.at[half, pl.ds(a * u, u)],
                a_place(x, h, k, a),
                at(x, y, 2 * l + half, k),
                a_sends + a * 2 + half,
                a_first + a * 2 + h,
            )

    def do_ao(a):
        arrived(a_place(x, h, k, a), a_first + a * 2 + h)
        ring_half(f"Ao{a}", a_place(x, h, k, a), x_right, x_left)
        to_sibling(a, 0, x, h)

    def do_am(a):
        arrived(a_place(x, 1 - h, k, a), a_first + a * 2 + 1 - h)
        ring_half(f"Am{a}", a_place(x, 1 - h, k, a), x_right, x_left)
        to_sibling(a, 1, x, 1 - h)

    def do_ar(a):
        wait(f"Ao{a}+")
        got[f"Af{a}+"] = push(a_place(x + 3, h, k, a), a_place(x + 3, h, k, a), x_right)
        to_sibling(a, 2, x + 3, h)

    def do_al(a):
        wait(f"Am{a}-")
        got[f"Af{a}-"] = push(a_place(x + 1, 1 - h, k, a), a_place(x + 1, 1 - h, k, a), x_left)
        to_sibling(a, 3, x + 1, 1 - h)

    def do_aq(a):
        wait(f"Ao{a}-", f"Am{a}+")
        to_sibling(a, 4, x + 1, h)
        to_sibling(a, 5, x + 3, 1 - h)

    def do_at(a):
        wait(f"Af{a}+", f"Af{a}-")
        for hh in range(2):
            to_sibling(a, 6 + hh, x + 2, hh)

    def do_ad(a):
        for i in range(8):
            wait(f"As{a}{i}")
        part = pl.ds(a * u, u)
        for xx in range(4):
            a_high[xx, part], a_low[xx, part] = split(a_all[xx, part])

    def do_fp(j):
        got[f"Fp{j}"] = push(f_send.at[j], f_place(j, z, k), sibling)

    def to_both(name, src):
        got[name + "m"] = push(src, src, z_mate)
        got[name + "o"] = push(src, src, z_outer)

    def do_fo(j):
        to_both(f"Fo{j}", f_place(j, z, k))

    def do_fm(j):
        wait(f"Fp{j}")
        to_both(f"Fm{j}", f_place(j, z, other))

    def f_block(j, zz):
        row = lax.div(zz, 2) * 2 * rows
        return f_all.at[j, pl.ds(mult(row, rows), 2 * rows), pl.ds(mult(lax.rem(zz, 2) * u, u), u)]

    def do_ff(j):
        wait(f"Fo{j}m", f"Fm{j}m")
        if j in BOTH_WAYS:
            got[f"Ff{j}+"] = push(f_place(j, mate, 0), f_place(j, mate, 0), z_outer)
            wait(f"Fo{j}o", f"Fm{j}o")
            got[f"Ff{j}-"] = push(f_place(j, outer, 1), f_place(j, outer, 1), z_mate)
        else:
            got[f"Ff{j}+"] = push(f_block(j, mate), f_block(j, mate), z_outer)

    def do_fd(j):
        wait(f"Ff{j}+", f"Ff{j}-" if j in BOTH_WAYS else f"Ff{j}+", f"Fo{j}o", f"Fm{j}o")
        f_high[j], f_low[j] = split(f_all[j])

    across, right, left = lax.rem(y + 2, 4), lax.rem(y + 1, 4), lax.rem(y + 3, 4)

    def sum_far(name, j, part, far, half):
        upper, lower = pl.ds(0, half), pl.ds(half, half)
        got[f"{name}{j}f+"] = push(part.at[j, across, upper], far.at[j, 0], y_right)
        got[f"{name}{j}f-"] = push(part.at[j, across, lower], far.at[j, 1], y_left)

    def sum_near(name, j, part, near, half):
        upper, lower = pl.ds(0, half), pl.ds(half, half)
        got[f"{name}{j}n+"] = push(part.at[j, right, lower], near.at[j, 0, lower], y_right)
        got[f"{name}{j}n-"] = push(part.at[j, left, upper], near.at[j, 1, upper], y_left)

    def sum_add(name, j, part, far, near, half):
        upper, lower = pl.ds(0, half), pl.ds(half, half)
        wait(f"{name}{j}f+")
        part[j, right, upper] = part[j, right, upper] + far[j, 0]
        got[f"{name}{j}a+"] = push(part.at[j, right, upper], near.at[j, 0, upper], y_right)
        wait(f"{name}{j}f-")
        part[j, left, lower] = part[j, left, lower] + far[j, 1]
        got[f"{name}{j}a-"] = push(part.at[j, left, lower], near.at[j, 1, lower], y_left)

    def total(name, j, part, near):
        wait(f"{name}{j}n+", f"{name}{j}n-", f"{name}{j}a+", f"{name}{j}a-")
        return part[j, y] + near[j, 0] + near[j, 1]

    def product1(c, blocks):
        j, part = c // 2, pl.ds((c % 2) * u, u)
        for block in blocks:
            p1[c, block] = dot3(a_high[block, part], a_low[block, part], f_high[j], f_low[j])

    def do_m1(c):
        product1(c, (across,))
        sum_far("R1", c, p1, far1, w)

    def do_m1r(c):
        product1(c, (right, left, y))
        sum_near("R1", c, p1, near1, w)

    def do_r1a(c):
        sum_add("R1", c, p1, far1, near1, w)

    z_first = fresh(2 * CHUNKS)
    z_send = fresh(2 * CHUNKS)
    g_first = fresh(4 * CHUNKS)
    g_send = fresh(4 * CHUNKS)

    def place_out(src, dst, lane, send, recv):
        move(jnp.logical_and(k == l, l == lane), src, dst, at(x, y, 2 * h + lane, l), send, recv)

    def do_t1(c):
        j, a = c // 2, c % 2
        value = -total("R1", c, p1, near1)
        z_own[j, pl.ds(a * u, u)] = value
        turned = jnp.transpose(value)
        for piece in range(4):
            z_turn[c, piece] = turned[piece * w : (piece + 1) * w]
        spot = z_all.at[j, x, :, pl.ds(mult(z * rows + a * u, u), u)]
        spot[...] = z_turn[c, z]
        for name, d in (("2", lax.rem(z + 2, 4)), ("m", mate), ("o", outer)):
            got[f"Zs{c}{name}"] = push(z_turn.at[c, d], spot, at(x, y, d, k))
        mine = f_all[j, pl.ds(mult(z * rows + a * u, u), u)]
        c_part[pl.ds(j, 1)] = c_part[pl.ds(j, 1)] - jnp.sum(value * mine, axis=0, keepdims=True)

    def do_zo(j):
        for lane in range(2):
            place_out(
                z_own.at[j, :, pl.ds(lane * u, u)],
                z_stage.at[k, j],
                lane,
                z_send + j * 2 + lane,
                z_first + k * CHUNKS + j,
            )

    def z_half(c, xx, half):
        return z_all.at[c // 2, lax.rem(xx, 4), pl.ds((c % 2) * (w // 2), w // 2), pl.ds(half * 4 * u, 4 * u)]

    def do_zn(c):
        wait(*(f"Zs{c // 2 * 2 + a}{name}" for a in range(2) for name in "2mo"))
        for half in range(2):
            ring_half(f"Zn{c}{half}", z_half(c, x, half), x_right, x_left)

    def do_zf(c):
        wait(f"Zn{c}0+")
        got[f"Zf{c}+"] = push(z_half(c, x + 3, 0), z_half(c, x + 3, 0), x_right)
        wait(f"Zn{c}1-")
        got[f"Zf{c}-"] = push(z_half(c, x + 1, 1), z_half(c, x + 1, 1), x_left)

    def do_zd(c):
        wait(f"Zn{c}1+", f"Zn{c}0-", f"Zf{c}+", f"Zf{c}-")
        v = w // 2
        for xx in range(4):
            part = z_all[c // 2, xx, pl.ds((c % 2) * v, v)]
            zh[c, pl.ds(xx * v, v)], zl[c, pl.ds(xx * v, v)] = split(part)

    def do_m2(c):
        v = w // 2
        for q in range(CHUNKS):
            value = dot3(zh[c], zl[c], f_high[q], f_low[q])
            for block in range(4):
                for lane in range(2):
                    p2[c, block, :, pl.ds((lane * CHUNKS + q) * u, u)] = value[
                        block * v : (block + 1) * v, lane * u : (lane + 1) * u
                    ]
        sum_far("R2", c, p2, far2, v // 2)
        sum_near("R2", c, p2, near2, v // 2)

    def do_r2a(c):
        sum_add("R2", c, p2, far2, near2, w // 4)

    def do_t2(c):
        g_own[c] = total("R2", c, p2, near2)
        for lane in range(2):
            place_out(
                g_own.at[c, :, pl.ds(lane * 4 * u, 4 * u)],
                g_stage.at[k, pl.ds(c * (w // 2), w // 2)],
                lane,
                g_send + c * 2 + lane,
                g_first + k * 2 * CHUNKS + c,
            )

    def prepare_diagonals():
        eye = lax.broadcasted_iota(jnp.int32, (rows, rows), 0) == lax.broadcasted_iota(jnp.int32, (rows, rows), 1)

        def diagonal(tile):
            return jnp.sum(jnp.where(eye, tile, 0.0), axis=0, keepdims=True)

        dd_send[...] = jnp.zeros_like(dd_send)
        dd_send[0, pl.ds(0, 1)] = diagonal(anc_ref[:, own_lanes])
        dd_send[1, pl.ds(0, 1)] = diagonal(diag_ref[other, :, own_lanes])
        dd_send[2, pl.ds(0, 1)] = diagonal(diag_ref[k, :, own_lanes])
        got["Da"] = push(dd_send.at[0], dd_recv.at[0], z_mate)
        got["Dd"] = push(dd_send.at[1], dd_recv.at[1], sibling)

    def start_sums():
        wait("Da", "Dd")
        zd[...] = jnp.where(l == h, dd_send[0], dd_recv[0])
        scale = jnp.logical_and(x == y, l == h).astype(f32)
        mine = dd_send[2, pl.ds(0, 1)]
        theirs = dd_recv[1, pl.ds(0, 1)]
        first = jnp.where(k == 0, mine, theirs) * scale
        last = jnp.where(k == 0, theirs, mine) * scale
        c_part[...] = jnp.zeros_like(c_part)
        for pair in range(2):
            woven = weave(first[:, pair * u : (pair + 1) * u], last[:, pair * u : (pair + 1) * u])
            for i in range(2):
                for lane in range(2):
                    c_part[pl.ds(2 * pair + i, 1), pl.ds(lane * u, u)] = woven[i] * (l == lane).astype(f32)

    def do_ca():
        for d in (1, 2, 3):
            got[f"Ca{d}"] = push(c_part, c_plane.at[d - 1], at(x, y, z + d, k))

    def do_cb():
        wait("Ca1", "Ca2", "Ca3")
        c_line[0] = c_part[...] + c_plane[0] + (c_plane[1] + c_plane[2])
        for d in (1, 2, 3):
            got[f"Cb{d}"] = push(c_line.at[0], c_line.at[d], at(x, y + d, z, k))

    def do_cc():
        wait("Cb1", "Cb2", "Cb3")
        c_front[...] = c_line[0] + c_line[1] + (c_line[2] + c_line[3])
        c_all[x, k] = c_front[...]
        got["Cc"] = push(c_front, c_all.at[x, k], sibling)

    def do_cd():
        wait("Cc")
        c_all[x, 2] = zd[...]
        for d in (1, 2, 3):
            got[f"Cd{d}"] = push(c_all.at[x], c_all.at[x], at(x + d, y, z, k))

    def columns(xx, front, lane):
        blocks = [c_all[xx, front, pl.ds(q, 1), pl.ds(mult(lane * u, u), u)] for q in range(CHUNKS)]
        woven = [weave(blocks[2 * pair], blocks[2 * pair + 1]) for pair in range(2)]
        return jnp.concatenate([woven[0][0], woven[1][0]], axis=1), jnp.concatenate([woven[0][1], woven[1][1]], axis=1)

    def prepare_edges():
        one_hot(u, near_ref, far_ref, hot_near, hot_far)
        bits = u.bit_length() - 1
        step = lax.broadcasted_iota(jnp.int32, (4 * u, near_ref.shape[1]), 0)
        column = ((step >> (bits - 1)) & 1) * 2 * u + (step >> bits) * w + (step & (w - 1))
        for front in range(2):
            near = near_ref[pl.ds(front, 1), :] - lax.axis_index("col") * 4 * u
            hot_stage[front] = (column == near).astype(f32).astype(jnp.bfloat16)

    def do_ce():
        wait("Cd1", "Cd2", "Cd3")
        for front in range(2):
            table[...] = jnp.zeros_like(table)
            first, last = columns(x, front, l)
            table[pl.ds(0, 1), pl.ds(0, rows)] = first
            table[pl.ds(0, 1), pl.ds(rows, rows)] = last
            near = pick(table[...], hot_near[front])
            first, last = columns(y, front, h)
            table[pl.ds(0, 1), pl.ds(0, rows)] = jnp.where(k == 0, first, last)
            table[pl.ds(0, 1), pl.ds(rows, rows)] = c_all[y, 2, pl.ds(0, 1)]
            far = pick(table[...], hot_far[front].astype(jnp.bfloat16))
            r_part[pl.ds(front, 1)] = near[0:1] + far[0:1]

    def finish_z():
        for front in range(2):
            for j in range(CHUNKS):
                arrived(z_stage.at[front, j], z_first + front * CHUNKS + j)
            for pair in range(2):
                woven = weave(z_stage[front, 2 * pair], z_stage[front, 2 * pair + 1])
                for i in range(2):
                    z_out[front, :, pl.ds((2 * i + pair) * u, u)] = woven[i]
            chosen = pick(z_out[front], hot_near[front]) * hot_far[front, pl.ds(rows, rows)]
            chosen = chosen + pick(diag_ref[front], hot_near[front]) * hot_far[front, pl.ds(0, rows)]
            r_part[pl.ds(front, 1)] = r_part[pl.ds(front, 1)] - 2.0 * jnp.sum(chosen, axis=0, keepdims=True)

    def finish_rows(first, last):
        v = w // 2
        part = pl.ds(first * v, (last - first) * v)
        for front in range(2):
            for c in range(first, last):
                arrived(g_stage.at[front, pl.ds(c * v, v)], g_first + front * 2 * CHUNKS + c)
            chosen = pick(g_stage[front, part], hot_stage[front]) * hot_far[front, part]
            r_part[pl.ds(front, 1)] = r_part[pl.ds(front, 1)] + 2.0 * jnp.sum(chosen, axis=0, keepdims=True)
            for pair in range(2):
                woven = weave(
                    g_stage[front, part, pl.ds(2 * pair * u, u)], g_stage[front, part, pl.ds((2 * pair + 1) * u, u)]
                )
                for i in range(2):
                    lanes = pl.ds((2 * i + pair) * u, u)
                    g_out[front, part, lanes] = diag_ref[front, part, lanes] - woven[i]

    def do_eg():
        finish_rows(0, 2 * CHUNKS - 2)

    steps = {
        "Ap": do_ap, "Ao": do_ao, "Am": do_am, "Ar": do_ar, "Al": do_al, "Aq": do_aq, "At": do_at, "Ad": do_ad,
        "Fp": do_fp, "Fo": do_fo, "Fm": do_fm, "Ff": do_ff, "Fd": do_fd,
        "M1": do_m1, "M1r": do_m1r, "R1a": do_r1a, "T1": do_t1,
        "Zo": do_zo, "Zn": do_zn, "Zf": do_zf, "Zd": do_zd,
        "M2": do_m2, "R2a": do_r2a, "T2": do_t2, "Da": prepare_diagonals,
        "Ds": start_sums, "Ed": prepare_edges, "Ca": do_ca, "Cb": do_cb, "Cc": do_cc, "Cd": do_cd, "Ce": do_ce,
        "Ez": finish_z, "Eg": do_eg,
    }
    loads[0].wait()
    turn_ancestor()
    pl.semaphore_wait(barrier, len(greet))
    for i, step in enumerate(ORDER):
        if i == 1:
            loads[1].wait()
            mask_factor()
            loads[2].wait()
        if step in steps:
            steps[step]()
        else:
            steps[step[:-1]](int(step[-1]))
    finish_rows(2 * CHUNKS - 2, 2 * CHUNKS)
    r_out[...] = r_part[0:2]

    for here, copy in moves:

        @pl.when(jnp.logical_not(here))
        def _():
            copy.wait_send()

    for copy in sent:
        copy.wait_send()


def per_device(anc_inverse, off_factor, diag_inverse, block_mask, edge_child, edge_other):
    fronts, rows, width = off_factor.shape
    edges = edge_child.shape[1]
    u = rows // 2
    w = u // 2
    n = CHUNKS
    f32, bf16 = jnp.float32, jnp.bfloat16
    vmem = pl.BlockSpec(memory_space=pltpu.VMEM)
    m, v = 2 * n, w // 2
    scratch = [
        ((n, rows, u), f32),
        ((n, 8 * u, 2 * u), f32),
        ((n, 8 * u, 2 * u), bf16),
        ((n, 8 * u, 2 * u), bf16),
        ((2, rows, rows), f32),
        ((4, rows, 8 * u), f32),
        ((4, rows, 8 * u), bf16),
        ((4, rows, 8 * u), bf16),
        ((m, 4, u, 2 * u), f32),
        ((m, 2, w, 2 * u), f32),
        ((m, 2, u, 2 * u), f32),
        ((n, rows, 2 * u), f32),
        ((m, 4, w, u), f32),
        ((n, 4, w, 8 * u), f32),
        ((m, 4 * v, 8 * u), bf16),
        ((m, 4 * v, 8 * u), bf16),
        ((2, n, rows, u), f32),
        ((m, 4, v, 8 * u), f32),
        ((m, 2, v // 2, 8 * u), f32),
        ((m, 2, v, 8 * u), f32),
        ((m, v, 8 * u), f32),
        ((2, rows, 4 * u), f32),
        ((3, 8, rows), f32),
        ((2, 8, rows), f32),
        ((8, rows), f32),
        ((3, 8, rows), f32),
        ((4, 8, rows), f32),
        ((8, rows), f32),
        ((4, 3, 8, rows), f32),
        ((8, rows), f32),
        ((8, 4 * u), f32),
        ((2, 4 * u, edges), bf16),
        ((2, 4 * u, edges), f32),
        ((2, 4 * u, edges), bf16),
        ((8, edges), f32),
        (anc_inverse.shape, f32),
        (off_factor.shape, f32),
        (diag_inverse.shape, f32),
    ]
    flops = 2 * 3 * 2 * (8 * u) ** 3
    wide = pltpu.VMEM((fronts, rows, width), f32)
    return pl.pallas_call(
        functools.partial(kernel, u),
        out_shape=(wide, wide, pltpu.VMEM((fronts, edges), f32)),
        in_specs=[pl.BlockSpec(memory_space=pltpu.SMEM)] + [pl.BlockSpec(memory_space=pl.ANY)] * 3 + [vmem] * 2,
        out_specs=(vmem, vmem, vmem),
        scratch_shapes=[pltpu.VMEM(*entry) for entry in scratch]
        + [pltpu.SemaphoreType.DMA((3,)), pltpu.SemaphoreType.DMA((SEMAPHORES,)), pltpu.SemaphoreType.DMA((SEMAPHORES,))],
        compiler_params=pltpu.CompilerParams(collective_id=0, has_side_effects=True, vmem_limit_bytes=54 << 20),
        cost_estimate=pl.CostEstimate(flops=flops, bytes_accessed=5 << 20, transcendentals=0),
    )(block_mask, anc_inverse, off_factor, diag_inverse, edge_child, edge_other)


def solution(mesh):
    placed = (
        P("row", "col"),
        P(None, "row", "col"),
        P(None, "row", "col"),
        P(None, "row"),
        P(None, ("row", "col")),
        P(None, ("row", "col")),
    )
    return jax.shard_map(
        per_device,
        mesh=mesh,
        in_specs=placed,
        out_specs=(P(None, "row", "col"), P(None, "row", "col"), P(None, ("row", "col"))),
        check_vma=False,
    )
```
